32 devices in a mesh: grp: 2 (over x), seq: 8 (over z, y), col: 2 (over core).
Axes of the slice: x: 2, y: 2, z: 4, core: 2. Of those that a mesh axis runs over, the one named last changes fastest.
Arguments:
- signal: bfloat16 [8192, 1408], P(('grp', 'seq'), 'col'), parts along dimension 0, may hold values from -6 to 6
- conv_weight: bfloat16 [5, 1408, 1408], P(None, None, 'col'), may hold values from -0.15625 to 0.15625
- conv_gain: float32 [1408], replicated, may hold values from 0.1 to 1.9
- embed_weight: bfloat16 [1408, 1536], P('col', 'seq'), may hold values from -0.15625 to 0.15625
- attn_gain: float32 [1536], replicated, may hold values from 0.1 to 1.9
- query_weight: bfloat16 [1536, 1024], P('seq'), may hold values from -4 to 4
- keyvalue_weight: bfloat16 [1536, 320], P('seq'), may hold values from -4 to 4
- output_weight: bfloat16 [1536, 1536], P(None, 'seq'), may hold values from -0.15625 to 0.15625
- rowcol_weight: bfloat16 [1536, 256], replicated, may hold values from -0.15625 to 0.15625
- pair_weight: bfloat16 [128, 128], replicated, may hold values from -0.5 to 0.5
Outputs:
- tokens: bfloat16 [2048, 1536], P(('grp', 'seq', 'col')), parts along dimension 0
- pair_out: bfloat16 [128, 64, 128], P(('grp', 'seq'), 'col'), parts along dimension 0
The draws below stay inside these ranges and needn't reach their ends.
There are 2 independent parts, one for each index of `grp`. The reference program is written for one: setup_inputs(seed, part) draws one part's arguments, and reference() takes and returns one part's arrays. A program takes and returns all parts, laid end to end along the dimension named above; an argument that names none is the same for every part. Nothing has to cross between parts.
All inputs are finite; a program needn't handle non-finite values.
Results may differ from the reference program's by a relative error of at most 0.015.
Values may be sent and summed in bfloat16 or wider, within the bound.
A program may use at most 128 MiB of HBM per device.

```python
import math
import jax
import jax.numpy as jnp
from jax import lax

C = 1408
D = 1536
H = 8
DK = 128
DV = 192
F = 128
TAPS = 5
POOL = 4
PAIR_POOL = 16
L = 4096


def key_matrix(key):
    return jax.random.truncated_normal(jax.random.fold_in(key, 11), -6.0, 6.0, (D, DK), jnp.float32) / math.sqrt(D)


def draw_keyvalue_weight(key, part):
    keys = key_matrix(key)
    values = jax.random.truncated_normal(jax.random.fold_in(key, 12), -6.0, 6.0, (D, DV), jnp.float32) / math.sqrt(D)
    return jnp.clip(jnp.concatenate([keys, values], axis=1), -4.0, 4.0).astype(jnp.bfloat16)


def draw_query_weight(key, part):
    noise = jax.random.truncated_normal(jax.random.fold_in(key, 13), -6.0, 6.0, (D, H * DK), jnp.float32) * (2.0 / math.sqrt(D))
    result = noise
    return jnp.clip(result, -4.0, 4.0).astype(jnp.bfloat16)


def block_scale(stream_key, shape, split, least, top_value):
    loudness = 1.0
    for dim, shards_of in split:
        heights = jax.random.uniform(jax.random.fold_in(jax.random.fold_in(stream_key, 6), dim), (shards_of,), jnp.float32, least / len(split), top_value / len(split))
        loudness = loudness * jnp.repeat(jnp.exp(heights), shape[dim] // shards_of).reshape((-1,) + (1,) * (len(shape) - 1 - dim))
    return loudness


def scatter_about(key, shape, scale, most, cuts=(), kind=jnp.bfloat16):
    gain = block_scale(key, shape, cuts, -0.22, 0.18) if cuts else 1.0
    values = jax.random.normal(key, shape, jnp.float32) * scale * gain
    return jnp.minimum(jnp.maximum(values, -most), most).astype(kind)


def setup_inputs(seed: int = 0, part: int = 0) -> dict:
    arg_keys = jax.random.split(jax.random.key(seed), 11)
    own_keys = jax.random.split(jax.random.fold_in(arg_keys[10], part), 11)
    return {
        "signal": scatter_about(own_keys[0], (L, C), 1.0, 6.0, ((0, 8), (1, 2))),
        "conv_weight": scatter_about(arg_keys[1], (TAPS, C, C), C ** -0.5, 0.15625, ((2, 2),)),
        "conv_gain": jnp.clip(1.0 + 0.18 * jax.random.normal(arg_keys[2], (C,), jnp.float32), 0.1, 1.9),
        "embed_weight": scatter_about(arg_keys[3], (C, D), C ** -0.5, 0.15625, ((0, 2), (1, 8))),
        "attn_gain": jnp.clip(1.0 + 0.18 * jax.random.normal(arg_keys[4], (D,), jnp.float32), 0.1, 1.9),
        "query_weight": draw_query_weight(jax.random.fold_in(arg_keys[10], 71), part),
        "keyvalue_weight": draw_keyvalue_weight(jax.random.fold_in(arg_keys[10], 71), part),
        "output_weight": scatter_about(arg_keys[7], (H * DV, D), (H * DV) ** -0.5, 0.15625, ((1, 8),)),
        "rowcol_weight": scatter_about(arg_keys[8], (D, 2 * F), D ** -0.5, 0.15625),
        "pair_weight": scatter_about(arg_keys[9], (F, F), F ** -0.5, 0.5),
    }


def rms_scale(values, gain_vector):
    return values * lax.rsqrt(lax.optimization_barrier(jnp.mean(values * values, axis=-1, keepdims=True)) + 1e-06) * gain_vector

def reference(signal, conv_weight, conv_gain, embed_weight, attn_gain, query_weight, keyvalue_weight, output_weight, rowcol_weight, pair_weight):
    length = signal.shape[0]
    features_in = signal.astype(jnp.float32)
    activated = jax.nn.gelu(rms_scale(features_in, conv_gain.astype(jnp.float32)), approximate=True).astype(jnp.bfloat16)
    half_width = TAPS // 2
    padded = jnp.pad(activated, ((half_width, half_width), (0, 0)))
    summed = features_in
    for tap_index in range(TAPS):
        summed = summed + jnp.dot(padded[tap_index:tap_index + length], conv_weight[tap_index], preferred_element_type=jnp.float32)
    pooled = lax.optimization_barrier(jnp.mean(summed.reshape(length // POOL, POOL, -1), axis=1)).astype(jnp.bfloat16)
    embedded = jnp.dot(pooled, embed_weight, preferred_element_type=jnp.float32).astype(jnp.bfloat16)
    normed = rms_scale(embedded.astype(jnp.float32), attn_gain.astype(jnp.float32)).astype(jnp.bfloat16)
    queries = (jnp.dot(normed, query_weight, preferred_element_type=jnp.float32) * DK ** (-0.5)).astype(jnp.bfloat16)
    keyvalue = jnp.dot(normed, keyvalue_weight, preferred_element_type=jnp.float32).astype(jnp.bfloat16)
    keys = keyvalue[:, :DK]
    values = keyvalue[:, DK:]
    token_count = queries.shape[0]
    per_head = jnp.transpose(queries.reshape(token_count, H, DK), (1, 0, 2))

    def one_head(head_queries):
        scores = lax.dot_general(head_queries, keys, (((1,), (1,)), ((), ())), preferred_element_type=jnp.float32)
        peak = lax.optimization_barrier(jnp.max(scores, axis=1, keepdims=True))
        weights = jnp.exp(scores - peak)
        total = lax.optimization_barrier(jnp.sum(weights, axis=1, keepdims=True))
        mixed = jnp.dot(weights.astype(jnp.bfloat16), values, preferred_element_type=jnp.float32) / total
        return mixed.astype(jnp.bfloat16)
    attended = lax.map(one_head, per_head)
    attended = jnp.transpose(attended, (1, 0, 2)).reshape(token_count, H * DV)
    attention_out = jnp.dot(attended, output_weight, preferred_element_type=jnp.float32)
    tokens = (embedded.astype(jnp.float32) + attention_out).astype(jnp.bfloat16)
    pair_pool = lax.optimization_barrier(jnp.mean(tokens.astype(jnp.float32).reshape(token_count // PAIR_POOL, PAIR_POOL, -1), axis=1)).astype(jnp.bfloat16)
    projected = jnp.dot(pair_pool, rowcol_weight, preferred_element_type=jnp.float32).astype(jnp.bfloat16)
    row_part = projected[:, :F].astype(jnp.float32)
    column_part = projected[:, F:].astype(jnp.float32)
    hidden = jax.nn.gelu(row_part[:, None, :] + column_part[None, :, :], approximate=True).astype(jnp.bfloat16)
    pair_rows = hidden.shape[0]
    pair_out = jnp.dot(hidden.reshape(-1, F), pair_weight, preferred_element_type=jnp.float32).astype(jnp.bfloat16)
    return (tokens, pair_out.reshape(pair_rows, pair_rows, F))
```

```python
import functools

import jax
import jax.numpy as jnp
from jax import lax
from jax.experimental import pallas as pl
from jax.experimental.pallas import tpu as pltpu
from jax.sharding import PartitionSpec as P

DK = 128
DV = 192
POOL = 4
PAIR_POOL = 16


def with_halo(array, sides, width):
    for axis, dim in sides:
        size, length = (lax.axis_size(axis), array.shape[dim])
        up = [(i, (i + 1) % size) for i in range(size - 1)]
        down = [(j, i) for i, j in up]
        last = lax.slice_in_dim(array, length - width, length, axis=dim)
        first = lax.slice_in_dim(array, 0, width, axis=dim)
        before = lax.ppermute(last, axis, up)
        after = lax.ppermute(first, axis, down)
        array = jnp.concatenate([before, array, after], axis=dim)
    return array


def rms_scale(values, gain_vector):
    return (
        values * lax.rsqrt(jnp.mean(values * values, axis=-1, keepdims=True) + 1e-06) * gain_vector
    )


def attention_parts(queries, head_count):
    query_rows = queries.reshape(queries.shape[0] * head_count, DK)

    def absorb(running, pieces, first_row):
        running_max, running_sum, accumulated = running
        key_piece, value_piece = pieces
        scores = lax.dot_general(
            query_rows, key_piece, (((1,), (1,)), ((), ())), preferred_element_type=jnp.float32
        )
        newest_max = jnp.maximum(running_max, jnp.max(scores, axis=1))
        weights = jnp.exp(scores - newest_max[:, None])
        running_sum = jnp.sum(weights, axis=1)
        accumulated = jnp.dot(
            weights.astype(jnp.bfloat16), value_piece, preferred_element_type=jnp.float32
        )
        return (newest_max, running_sum, accumulated)

    row_count = query_rows.shape[0]
    initial = (
        jnp.full((row_count,), -1e30, jnp.float32),
        jnp.zeros((row_count,), jnp.float32),
        jnp.zeros((row_count, DV), jnp.float32),
    )
    return (absorb, initial)


def finish_attention(result, token_count):
    running_max, running_sum, accumulated = result
    return (accumulated / running_sum[:, None]).astype(jnp.bfloat16).reshape(token_count, -1)


def on_device(
    signal,
    conv_weight,
    conv_gain,
    embed_weight,
    attn_gain,
    query_weight,
    keyvalue_weight,
    output_weight,
    rowcol_weight,
    pair_weight,
):
    positions = signal.shape[0]
    tap_count = conv_weight.shape[0]
    halo_width = tap_count // 2
    padded = with_halo(signal, (("seq", 0),), halo_width)
    widened = lax.all_gather(padded, "col", axis=1, tiled=True)
    activated = jax.nn.gelu(
        rms_scale(widened.astype(jnp.float32), conv_gain), approximate=True
    ).astype(jnp.bfloat16)
    summed = signal.astype(jnp.float32)
    for tap_index in range(tap_count):
        summed = summed + jnp.dot(
            activated[tap_index : tap_index + positions],
            conv_weight[tap_index],
            preferred_element_type=jnp.float32,
        )
    pooled = jnp.mean(summed.reshape(positions // POOL, POOL, -1), axis=1).astype(jnp.bfloat16)
    embed_full = lax.all_gather(embed_weight, "seq", axis=1, tiled=True)
    col_count = lax.axis_size("col")
    embedded = lax.psum_scatter(
        jnp.dot(pooled, embed_full, preferred_element_type=jnp.float32).astype(jnp.bfloat16),
        "col",
        scatter_dimension=0,
        tiled=True,
    )
    normed = rms_scale(embedded.astype(jnp.float32), attn_gain).astype(jnp.bfloat16)
    head_count = query_weight.shape[1] // DK
    scaling = DK ** (-0.5)
    col_index = lax.axis_index("col")
    local_heads = head_count // col_count
    group_tokens = lax.all_gather(normed, "col", axis=0, tiled=True)
    group_count = group_tokens.shape[0]
    query_half = lax.dynamic_slice_in_dim(
        query_weight, col_index * local_heads * DK, local_heads * DK, 1
    )
    query_sum = jnp.dot(
        group_tokens,
        lax.all_gather(query_half, "seq", axis=0, tiled=True),
        preferred_element_type=jnp.float32,
    )
    keyvalue_sum = jnp.dot(
        group_tokens,
        lax.all_gather(keyvalue_weight, "seq", axis=0, tiled=True),
        preferred_element_type=jnp.float32,
    )
    queries = (query_sum * scaling).astype(jnp.bfloat16)
    keyvalue = keyvalue_sum.astype(jnp.bfloat16)
    absorb, initial = attention_parts(queries, local_heads)
    result = absorb(
        initial,
        (
            lax.all_gather(keyvalue[:, :DK], "seq", axis=0, tiled=True),
            lax.all_gather(keyvalue[:, DK:], "seq", axis=0, tiled=True),
        ),
        jnp.int32(0),
    )
    attended = finish_attention(result, group_count)
    output_half = lax.dynamic_slice_in_dim(
        output_weight, col_index * local_heads * DV, local_heads * DV, 0
    )
    partial_out = jnp.dot(
        attended,
        lax.all_gather(output_half, "seq", axis=1, tiled=True),
        preferred_element_type=jnp.float32,
    )
    attention_out = lax.psum_scatter(
        partial_out.astype(jnp.bfloat16), "col", scatter_dimension=0, tiled=True
    ).astype(jnp.float32)
    tokens = (embedded.astype(jnp.float32) + attention_out).astype(jnp.bfloat16)
    pair_pool = jnp.mean(
        tokens.astype(jnp.float32).reshape(-1, PAIR_POOL, tokens.shape[1]), axis=1
    ).astype(jnp.bfloat16)
    projected = jnp.dot(pair_pool, rowcol_weight, preferred_element_type=jnp.float32).astype(
        jnp.bfloat16
    )
    features = pair_weight.shape[0]
    row_block = lax.all_gather(projected, "col", axis=0, tiled=True)
    column_all = lax.all_gather(row_block[:, features:], "seq", axis=0, tiled=True)
    row_part = row_block[:, :features]
    column_span = column_all.shape[0] // col_count
    column_part = lax.dynamic_slice_in_dim(
        column_all, lax.axis_index("col") * column_span, column_span, 0
    )
    hidden = jax.nn.gelu(
        row_part.astype(jnp.float32)[:, None, :] + column_part.astype(jnp.float32)[None, :, :],
        approximate=True,
    ).astype(jnp.bfloat16)
    pair_out = jnp.dot(
        hidden.reshape(-1, features), pair_weight, preferred_element_type=jnp.float32
    ).astype(jnp.bfloat16)
    return (tokens, pair_out.reshape(row_part.shape[0], column_span, features))


EDGE = 16
Y = 2
PIECES = (2, 1, 2, 2)


def fused_kernel(
    taps,
    heads,
    signal,
    conv_w,
    conv_gain,
    embed_w,
    attn_gain,
    query_w,
    kv_w,
    out_w,
    rowcol,
    pair_w,
    tokens_out,
    pair_out,
    sig,
    act,
    win,
    edge,
    halo,
    conv_buf,
    e_buf,
    q_buf,
    k_buf,
    o_buf,
    rc_buf,
    pools,
    part,
    other,
    emb,
    normed,
    ssq,
    scales,
    kv_part,
    q_part,
    kv_all,
    att,
    tok_peer,
    cols,
    rows_peer,
    hid,
    loc_sem,
    send_sem,
    recv_sem,
):
    f32, bf16 = jnp.float32, jnp.bfloat16
    n = lax.axis_size("seq")
    nz = n // Y
    s = lax.axis_index("seq")
    c = lax.axis_index("col")
    x = lax.axis_index("grp")
    z, y = s // Y, s % Y
    half = sig.shape[1]
    positions = sig.shape[2]
    count = positions // POOL
    width = e_buf.shape[1]
    halo_width = taps // 2
    started = []
    local = []

    def remote(src, dst, to):
        index = len(started)
        copy = pltpu.make_async_remote_copy(
            src_ref=src,
            dst_ref=dst,
            send_sem=send_sem.at[index],
            recv_sem=recv_sem.at[index],
            device_id=to,
            device_id_type=pl.DeviceIdType.MESH,
        )
        copy.start()
        started.append(copy)
        return copy

    def fetch(src, dst):
        copy = pltpu.make_async_copy(src, dst, loc_sem.at[len(local)])
        copy.start()
        local.append(copy)
        return copy

    def seq_of(z_index, y_index):
        return z_index * Y + y_index

    def z_from(dz):
        return (z + nz - dz) % nz

    def z_to(dz):
        return (z + dz) % nz

    partner = {"col": 1 - c}
    y_peer = {"seq": seq_of(z, 1 - y)}
    x_peer = {"grp": 1 - x}
    z_next = {"seq": seq_of(z_to(1), y)}

    sig_here = fetch(signal, sig.at[0])
    barrier = pltpu.get_barrier_semaphore()
    for d in range(n):
        for e in range(2):
            if d or e:
                pl.semaphore_signal(
                    barrier,
                    inc=1,
                    device_id={"seq": (s + d) % n, "col": (c + e) % 2},
                    device_id_type=pl.DeviceIdType.MESH,
                )
    pl.semaphore_signal(barrier, inc=1, device_id=x_peer, device_id_type=pl.DeviceIdType.MESH)

    k_rows = kv_w.shape[0] // 2
    q_cols = query_w.shape[1] // 2
    o_cols = out_w.shape[1] // 2
    kv_own = kv_w.at[pl.ds(pl.multiple_of(c * k_rows, 16), k_rows)]
    q_own = query_w.at[:, pl.ds(pl.multiple_of(c * q_cols, 128), q_cols)]
    o_own = out_w.at[:, pl.ds(pl.multiple_of(c * o_cols, 128), o_cols)]

    def k_at(owner):
        return k_buf.at[owner, pl.ds(pl.multiple_of(c * k_rows, 16), k_rows)]

    weights = [
        (embed_w, lambda owner: e_buf.at[owner]),
        (kv_own, k_at),
        (q_own, lambda owner: q_buf.at[owner]),
        (o_own, lambda owner: o_buf.at[owner]),
    ]
    E, KV, Q, O = range(4)
    conv_here = [fetch(conv_w.at[t], conv_buf.at[t]) for t in range(taps)]
    own_here = [fetch(own, at(z)) for own, at in weights]
    rc_here = []
    for k in range(nz):
        rows = pl.ds(pl.multiple_of(seq_of(k, y) * width, 16), width)
        rc_here.append(fetch(rowcol.at[rows], rc_buf.at[k]))

    row = lax.broadcasted_iota(jnp.int32, (EDGE, positions), 0)
    place = lax.broadcasted_iota(jnp.int32, (EDGE, positions), 1)
    wanted = jnp.where(row < EDGE // 2, row, row - EDGE // 2 + positions - halo_width)
    in_use = lax.rem(row, EDGE // 2) < halo_width
    pick = jnp.where((place == wanted) & in_use, 1.0, 0.0).astype(bf16)
    sig_here.wait()
    over_rows = (((1,), (1,)), ((), ()))
    edge[...] = lax.dot_general(pick, sig[0], over_rows, preferred_element_type=f32).astype(bf16)

    pl.semaphore_wait(barrier, 2 * n)

    signal_copy = remote(signal, sig.at[1], partner)
    copies = {}

    def piece(ref, w, p):
        rows = ref.shape[0] // 2 // PIECES[w]
        return ref.at[pl.ds(pl.multiple_of((x * PIECES[w] + p) * rows, 16), rows)]

    def begin(w):
        own, at = weights[w]
        for p in range(PIECES[w]):
            copies[w, p, "z", 1] = remote(piece(own, w, p), piece(at(z), w, p), z_next)

    def hop(w, dz):
        _, at = weights[w]
        for p in range(PIECES[w]):
            copies[w, p, "z", dz].wait_recv()
            ref = piece(at(z_from(dz)), w, p)
            if dz + 1 < nz:
                copies[w, p, "z", dz + 1] = remote(ref, ref, z_next)
            copies[w, p, "x", dz] = remote(ref, ref, x_peer)

    def arrived(w, dz):
        if dz == 0:
            own_here[w].wait()
        else:
            for p in range(PIECES[w]):
                copies[w, p, "x", dz].wait_recv()

    begin(E)
    halo_copies = []
    for e in range(2):
        core = (c + e) % 2
        up = {"seq": (s + 1) % n, "col": core}
        down = {"seq": (s + n - 1) % n, "col": core}
        halo_copies.append(remote(edge, halo.at[e, 0], up))
        halo_copies.append(remote(edge, halo.at[e, 1], down))
    begin(KV)
    begin(Q)

    def windows(position):
        column = lax.broadcasted_iota(jnp.int32, position.shape, 1)
        tap = column // count
        begin = (column - tap * count) * POOL + tap - halo_width
        hit = (position >= begin) & (position < begin + POOL)
        return jnp.where(hit, 1.0 / POOL, 0.0).astype(bf16)

    mean_of = windows(lax.broadcasted_iota(jnp.int32, (positions, taps * count), 0))
    edge_row = lax.broadcasted_iota(jnp.int32, (EDGE, taps * count), 0)
    edge_means = [windows(edge_row - EDGE // 2 - halo_width), windows(edge_row + positions)]
    edge_means = [
        jnp.where((edge_row >= EDGE // 2) & (s > 0), edge_means[0], 0.0).astype(bf16),
        jnp.where((edge_row < EDGE // 2) & (s < n - 1), edge_means[1], 0.0).astype(bf16),
    ]
    channels = 2 * half
    gains = [conv_gain[pl.ds(c, 1), :], conv_gain[pl.ds(1 - c, 1), :]]
    gain_columns = [jnp.broadcast_to(g, (128, half)).T for g in gains]

    signal_copy.wait_recv()

    block = 64
    square = jnp.zeros((1, positions), f32)
    for h in range(2):
        v = sig[h].astype(f32)
        square = square + jnp.sum(v * v, axis=0, keepdims=True)
    scale = lax.rsqrt(square * (1.0 / channels) + 1e-06)
    for h in range(2):
        for i in range(half // block):
            rows = slice(i * block, (i + 1) * block)
            v = sig[h, rows, :].astype(f32) * scale * gain_columns[h][rows, :1]
            act[h, rows, :] = jax.nn.gelu(v, approximate=True).astype(bf16)

    hop(E, 1)
    for copy in halo_copies:
        copy.wait_recv()

    edges = [[], []]
    for side in range(2):
        a, b = halo[0, side].astype(f32), halo[1, side].astype(f32)
        square = jnp.sum(a * a, axis=1, keepdims=True) + jnp.sum(b * b, axis=1, keepdims=True)
        edge_scale = lax.rsqrt(square * (1.0 / channels) + 1e-06)
        for h, v in enumerate((a, b)):
            v = jax.nn.gelu(v * edge_scale * gains[h], approximate=True)
            edges[h].append(v.T.astype(bf16))
    for h in range(2):
        core = c if h == 0 else 1 - c
        mean = jnp.dot(act[h], mean_of, preferred_element_type=f32)
        for side in range(2):
            mean = mean + jnp.dot(edges[h][side], edge_means[side], preferred_element_type=f32)
        win[pl.ds(pl.multiple_of(core * half, 16), half), :] = mean.astype(bf16)

    hop(E, 2)
    hop(KV, 1)

    middle = slice(halo_width * count, (halo_width + 1) * count)
    for copy in conv_here:
        copy.wait()
    chunks = 2
    size = half // chunks
    pool_copies = []
    for i in range(chunks):
        rows = slice(i * size, (i + 1) * size)
        total = jnp.dot(sig[0, rows, :], mean_of[:, middle], preferred_element_type=f32)
        for t in range(taps):
            total = total + jnp.dot(
                conv_buf[t, rows, :],
                win[:, t * count : (t + 1) * count],
                preferred_element_type=f32,
            )
        pools[0, rows, :] = total.astype(bf16)
        span = pl.ds(i * size, size)
        pool_copies.append(remote(pools.at[0, span], pools.at[1, span], y_peer))
        if i == 0:
            hop(E, 3)
            hop(KV, 2)
            hop(Q, 1)

    hop(KV, 3)
    begin(O)
    hop(Q, 2)
    for copy in pool_copies:
        copy.wait_recv()
    both = jnp.concatenate([pools[0], pools[1]], axis=1)
    swaps = []
    for dz in range(nz):
        owner = z_from(dz)
        arrived(E, dz)
        part[0, owner] = jnp.dot(e_buf[owner], both, preferred_element_type=f32).astype(bf16)
        swaps.append(remote(part.at[0, owner], other.at[0, owner], partner))
    passed = []
    for dz in range(nz):
        arrived(KV, dz)
        ref = k_at(z_from(dz))
        passed.append(remote(ref, ref, partner))
    hop(Q, 3)
    hop(O, 1)
    gain_of = []
    for j in range(Y):
        blocks = [attn_gain[:, (k * Y + j) * width : (k * Y + j + 1) * width] for k in range(nz)]
        gain_of.append(jnp.concatenate(blocks, axis=1))
    gain_row = jnp.where(y == 0, gain_of[0], gain_of[1])
    for copy in swaps:
        copy.wait_recv()
    square = jnp.zeros((1, 2 * count), f32)
    for k in range(0, nz, 2):
        columns = slice(k * width, (k + 2) * width)
        pair = []
        for b in (k, k + 1):
            v = (part[0, b].astype(f32) + other[0, b].astype(f32)).astype(bf16)
            emb[b] = v
            v = v.astype(f32)
            square = square + jnp.sum(v * v, axis=0, keepdims=True)
            pair.append(v)
        v = jnp.concatenate(pair, axis=0).T
        normed[:, columns] = (v * gain_row[:, columns]).astype(bf16)
    ssq[0] = jnp.broadcast_to(square[:, count:], (8, count))
    ssq_copy = remote(ssq.at[0], ssq.at[1], y_peer)

    own_half = pl.ds(pl.multiple_of(c * (count // 2), 16), count // 2)
    peer_half = pl.ds(pl.multiple_of(count + c * (count // 2), 16), count // 2)
    for copy in passed:
        copy.wait_recv()
    kv = jnp.dot(
        jnp.concatenate([normed[own_half, :], normed[peer_half, :]], axis=0),
        k_buf[...].reshape(nz * width, k_buf.shape[2]),
        preferred_element_type=f32,
    )
    kv_part[0] = kv[count // 2 :].astype(bf16)
    kv_swap = remote(kv_part.at[0], kv_part.at[1], y_peer)
    for dz in range(nz):
        arrived(Q, dz)
    queries = jnp.dot(
        normed[...], q_buf[...].reshape(nz * width, q_cols), preferred_element_type=f32
    )
    q_part[0] = queries[count:].astype(bf16)
    q_swap = remote(q_part.at[0], q_part.at[1], y_peer)

    ssq_copy.wait_recv()
    square = square[:, :count] + ssq[1, 0:1, :]
    scale = lax.rsqrt(square * (1.0 / (n * width)) + 1e-06)
    scales[...] = jnp.broadcast_to(scale, (128, count)).T

    def kv_at(owner):
        return kv_all.at[owner, own_half]

    kv_swap.wait_recv()
    kv = (kv[: count // 2] + kv_part[1].astype(f32)) * scales[own_half, :1]
    kv_all[s, own_half, :] = kv.astype(bf16)
    mine = kv_at(s)
    kv_copies = {}
    for dz in (2, 1, 3):
        kv_copies["z", dz] = remote(mine, mine, {"seq": seq_of(z_to(dz), y)})
    kv_copies["y", 0] = remote(mine, mine, y_peer)
    across = [remote(mine, mine, partner)]
    hop(O, 2)
    q_swap.wait_recv()
    queries = (queries[:count] + q_part[1].astype(f32)) * (scales[:, :1] * (DK**-0.5))
    queries = queries.astype(bf16)
    for dz in (1, 3, 2):
        kv_copies["z", dz].wait_recv()
        ref = kv_at(seq_of(z_from(dz), y))
        kv_copies["y", dz] = remote(ref, ref, y_peer)
        across.append(remote(ref, ref, partner))
    for dz in (0, 1, 3, 2):
        kv_copies["y", dz].wait_recv()
        ref = kv_at(seq_of(z_from(dz), 1 - y))
        across.append(remote(ref, ref, partner))
    hop(O, 3)
    for copy in across:
        copy.wait_recv()

    everything = kv_all[...].reshape(n * count, kv_all.shape[2])
    keys, values = everything[:, :DK], everything[:, DK:]
    att_copies = []
    for h in range(0, heads, 2):
        mixes = []
        for i in (h, h + 1):
            scores = lax.dot_general(
                queries[:, i * DK : (i + 1) * DK],
                keys,
                over_rows,
                preferred_element_type=f32,
            )
            exps = jnp.exp(scores - jnp.max(scores, axis=1, keepdims=True))
            norm = jnp.sum(exps, axis=1, keepdims=True)
            mixed = jnp.dot(exps.astype(bf16), values, preferred_element_type=f32)
            mixes.append((mixed / norm).astype(bf16))
        att[0, :, h * DV : (h + 2) * DV] = jnp.concatenate(mixes, axis=1)
        span = pl.ds(h * DV, 2 * DV)
        att_copies.append(remote(att.at[0, :, span], att.at[1, :, span], y_peer))

    for dz in range(nz):
        arrived(O, dz)
    tokens = []
    rows_n = count // PAIR_POOL
    features = pair_w.shape[0]
    for j in range(Y):
        if j:
            for copy in att_copies:
                copy.wait_recv()
        span = slice(j * count, (j + 1) * count)
        acc = lax.dot_general(
            o_buf[...].reshape(nz * width, o_cols), att[j], over_rows, preferred_element_type=f32
        )
        part[1, :, :, span] = acc.reshape(nz, width, count).astype(bf16)
        there = pl.ds(j * count, count)
        tokens.append(remote(part.at[1, :, :, there], other.at[1, :, :, there], partner))
    for j in range(Y):
        tokens[j].wait_recv()
        span = slice(j * count, (j + 1) * count)
        for k in range(0, nz, 2):
            columns = slice(k * width, (k + 2) * width)
            pair = [
                emb[b, :, span].astype(f32)
                + (part[1, b, :, span].astype(f32) + other[1, b, :, span].astype(f32))
                for b in (k, k + 1)
            ]
            normed[span, columns] = jnp.concatenate(pair, axis=0).T.astype(bf16)
    tok_copy = remote(normed.at[peer_half], tok_peer, y_peer)
    row_of = lax.broadcasted_iota(jnp.int32, (2 * rows_n, 2 * count), 0)
    token_of = lax.broadcasted_iota(jnp.int32, (2 * rows_n, 2 * count), 1) // PAIR_POOL
    pool = jnp.where(row_of == token_of, 1.0 / PAIR_POOL, 0.0).astype(bf16)
    for copy in rc_here:
        copy.wait()
    pair_pool = jnp.dot(pool, normed[...], preferred_element_type=f32).astype(bf16)
    projected = jnp.dot(
        pair_pool, rc_buf[...].reshape(nz * width, 2 * features), preferred_element_type=f32
    )
    cols[s] = projected[:, features:].astype(bf16)
    rows_peer[0] = projected[:, :features].astype(bf16)
    rows_copy = remote(rows_peer.at[0], rows_peer.at[1], y_peer)
    col_copies = []
    for d in range(1, n):
        to = {"seq": (s + d) % n}
        col_copies.append(remote(cols.at[s], cols.at[s], to))
    rows_copy.wait_recv()
    row_part = projected[:rows_n, :features] + rows_peer[1].astype(f32)[rows_n:]
    row_part = row_part.astype(bf16).astype(f32)[:, None, :]
    tok_copy.wait_recv()
    tok_own, tok_other = normed[own_half, :], tok_peer[...]
    for k in range(nz):
        a = tok_own[:, k * width : (k + 1) * width]
        b = tok_other[:, k * width : (k + 1) * width]
        pair = [jnp.where(y == 0, a, b), jnp.where(y == 0, b, a)]
        tokens_out[:, k * 2 * width : (k + 1) * 2 * width] = jnp.concatenate(pair, axis=1)
    for copy in col_copies:
        copy.wait_recv()
    for j in range(nz // 2):
        both = [cols[c * (n // 2) + Y * j + i].astype(f32) for i in range(Y)]
        for i in range(Y):
            column = both[i][:rows_n] + both[1 - i][rows_n:]
            column = column.astype(bf16).astype(f32)
            hid[:, pl.ds((Y * j + i) * rows_n, rows_n), :] = jax.nn.gelu(
                row_part + column[None, :, :], approximate=True
            )
    hidden = hid[...].reshape(rows_n * (n // 2) * rows_n, features).astype(bf16)
    result = jnp.dot(hidden, pair_w[...], preferred_element_type=f32)
    pair_out[...] = result.reshape(pair_out.shape).astype(bf16)
    for copy in started:
        copy.wait_send()


def on_device_fused(
    signal,
    conv_weight,
    conv_gain,
    embed_weight,
    attn_gain,
    query_weight,
    keyvalue_weight,
    output_weight,
    rowcol_weight,
    pair_weight,
):
    bf16, f32 = jnp.bfloat16, jnp.float32
    n = lax.axis_size("seq")
    nz = n // Y
    positions, half = signal.shape
    taps, channels, _ = conv_weight.shape
    count = positions // POOL
    width = embed_weight.shape[1]
    q_cols = query_weight.shape[1] // 2
    heads = q_cols // DK
    kv_cols = keyvalue_weight.shape[1]
    rows_n = count // PAIR_POOL
    features = pair_weight.shape[0]
    any_spec = pl.BlockSpec(memory_space=pl.ANY)
    vmem = pl.BlockSpec(memory_space=pltpu.VMEM)
    dma = pltpu.SemaphoreType.DMA
    tokens, pair = pl.pallas_call(
        functools.partial(fused_kernel, taps, heads),
        out_shape=(
            jax.ShapeDtypeStruct((count // 2, n * width), bf16),
            jax.ShapeDtypeStruct((rows_n, rows_n * n // 2, features), bf16),
        ),
        in_specs=[any_spec, any_spec, vmem, any_spec, vmem]
        + [any_spec, any_spec, any_spec, any_spec, vmem],
        out_specs=(vmem, vmem),
        scratch_shapes=[
            pltpu.VMEM((2, half, positions), bf16),
            pltpu.VMEM((2, half, positions), bf16),
            pltpu.VMEM((2 * half, taps * count), bf16),
            pltpu.VMEM((EDGE, half), bf16),
            pltpu.VMEM((2, 2, EDGE, half), bf16),
            pltpu.VMEM((taps, half, channels), bf16),
            pltpu.VMEM((nz, width, half), bf16),
            pltpu.VMEM((nz, width, q_cols), bf16),
            pltpu.VMEM((nz, width, kv_cols), bf16),
            pltpu.VMEM((nz, width, heads * DV), bf16),
            pltpu.VMEM((nz, width, 2 * features), bf16),
            pltpu.VMEM((2, half, count), bf16),
            pltpu.VMEM((2, nz, width, 2 * count), bf16),
            pltpu.VMEM((2, nz, width, 2 * count), bf16),
            pltpu.VMEM((nz, width, 2 * count), bf16),
            pltpu.VMEM((2 * count, nz * width), bf16),
            pltpu.VMEM((2, 8, count), f32),
            pltpu.VMEM((count, 128), f32),
            pltpu.VMEM((2, count // 2, kv_cols), bf16),
            pltpu.VMEM((2, count, q_cols), bf16),
            pltpu.VMEM((n, count, kv_cols), bf16),
            pltpu.VMEM((2, count, heads * DV), bf16),
            pltpu.VMEM((count // 2, nz * width), bf16),
            pltpu.VMEM((n, 2 * rows_n, features), bf16),
            pltpu.VMEM((2, 2 * rows_n, features), bf16),
            pltpu.VMEM((rows_n, rows_n * n // 2, features), f32),
            dma((32,)),
            dma((160,)),
            dma((160,)),
        ],
        compiler_params=pltpu.CompilerParams(
            collective_id=0, has_side_effects=True, vmem_limit_bytes=60 * 1024 * 1024
        ),
    )(
        signal.T,
        jnp.swapaxes(conv_weight, 1, 2),
        conv_gain.reshape(2, half),
        embed_weight.T,
        attn_gain.reshape(1, n * width),
        query_weight,
        keyvalue_weight,
        output_weight.T,
        rowcol_weight,
        pair_weight,
    )
    return tokens, pair


def fits(mesh):
    n = mesh.shape["seq"]
    return n == 8 and mesh.shape["col"] == 2 and mesh.shape["grp"] == 2


def solution(mesh):
    placed = (
        P(("grp", "seq"), "col"),
        P(None, None, "col"),
        P(),
        P("col", "seq"),
        P(),
        P("seq", None),
        P("seq", None),
        P(None, "seq"),
        P(),
        P(),
    )
    return jax.shard_map(
        on_device_fused if fits(mesh) else on_device,
        mesh=mesh,
        in_specs=placed,
        out_specs=(P(("grp", "seq", "col"), None), P(("grp", "seq"), "col", None)),
        check_vma=False,
    )
```

```python
import functools

import jax
import jax.numpy as jnp
from jax import lax
from jax.experimental import pallas as pl
from jax.experimental.pallas import tpu as pltpu
from jax.sharding import PartitionSpec as P

DK = 128
DV = 192
POOL = 4
PAIR_POOL = 16


def with_halo(array, sides, width):
    for axis, dim in sides:
        size, length = (lax.axis_size(axis), array.shape[dim])
        up = [(i, (i + 1) % size) for i in range(size - 1)]
        down = [(j, i) for i, j in up]
        last = lax.slice_in_dim(array, length - width, length, axis=dim)
        first = lax.slice_in_dim(array, 0, width, axis=dim)
        before = lax.ppermute(last, axis, up)
        after = lax.ppermute(first, axis, down)
        array = jnp.concatenate([before, array, after], axis=dim)
    return array


def rms_scale(values, gain_vector):
    return (
        values * lax.rsqrt(jnp.mean(values * values, axis=-1, keepdims=True) + 1e-06) * gain_vector
    )


def attention_parts(queries, head_count):
    query_rows = queries.reshape(queries.shape[0] * head_count, DK)

    def absorb(running, pieces, first_row):
        running_max, running_sum, accumulated = running
        key_piece, value_piece = pieces
        scores = lax.dot_general(
            query_rows, key_piece, (((1,), (1,)), ((), ())), preferred_element_type=jnp.float32
        )
        newest_max = jnp.maximum(running_max, jnp.max(scores, axis=1))
        weights = jnp.exp(scores - newest_max[:, None])
        running_sum = jnp.sum(weights, axis=1)
        accumulated = jnp.dot(
            weights.astype(jnp.bfloat16), value_piece, preferred_element_type=jnp.float32
        )
        return (newest_max, running_sum, accumulated)

    row_count = query_rows.shape[0]
    initial = (
        jnp.full((row_count,), -1e30, jnp.float32),
        jnp.zeros((row_count,), jnp.float32),
        jnp.zeros((row_count, DV), jnp.float32),
    )
    return (absorb, initial)


def finish_attention(result, token_count):
    running_max, running_sum, accumulated = result
    return (accumulated / running_sum[:, None]).astype(jnp.bfloat16).reshape(token_count, -1)


def on_device(
    signal,
    conv_weight,
    conv_gain,
    embed_weight,
    attn_gain,
    query_weight,
    keyvalue_weight,
    output_weight,
    rowcol_weight,
    pair_weight,
):
    positions = signal.shape[0]
    tap_count = conv_weight.shape[0]
    halo_width = tap_count // 2
    padded = with_halo(signal, (("seq", 0),), halo_width)
    widened = lax.all_gather(padded, "col", axis=1, tiled=True)
    activated = jax.nn.gelu(
        rms_scale(widened.astype(jnp.float32), conv_gain), approximate=True
    ).astype(jnp.bfloat16)
    summed = signal.astype(jnp.float32)
    for tap_index in range(tap_count):
        summed = summed + jnp.dot(
            activated[tap_index : tap_index + positions],
            conv_weight[tap_index],
            preferred_element_type=jnp.float32,
        )
    pooled = jnp.mean(summed.reshape(positions // POOL, POOL, -1), axis=1).astype(jnp.bfloat16)
    embed_full = lax.all_gather(embed_weight, "seq", axis=1, tiled=True)
    col_count = lax.axis_size("col")
    embedded = lax.psum_scatter(
        jnp.dot(pooled, embed_full, preferred_element_type=jnp.float32).astype(jnp.bfloat16),
        "col",
        scatter_dimension=0,
        tiled=True,
    )
    normed = rms_scale(embedded.astype(jnp.float32), attn_gain).astype(jnp.bfloat16)
    head_count = query_weight.shape[1] // DK
    scaling = DK ** (-0.5)
    col_index = lax.axis_index("col")
    local_heads = head_count // col_count
    group_tokens = lax.all_gather(normed, "col", axis=0, tiled=True)
    group_count = group_tokens.shape[0]
    query_half = lax.dynamic_slice_in_dim(
        query_weight, col_index * local_heads * DK, local_heads * DK, 1
    )
    query_sum = jnp.dot(
        group_tokens,
        lax.all_gather(query_half, "seq", axis=0, tiled=True),
        preferred_element_type=jnp.float32,
    )
    keyvalue_sum = jnp.dot(
        group_tokens,
        lax.all_gather(keyvalue_weight, "seq", axis=0, tiled=True),
        preferred_element_type=jnp.float32,
    )
    queries = (query_sum * scaling).astype(jnp.bfloat16)
    keyvalue = keyvalue_sum.astype(jnp.bfloat16)
    absorb, initial = attention_parts(queries, local_heads)
    result = absorb(
        initial,
        (
            lax.all_gather(keyvalue[:, :DK], "seq", axis=0, tiled=True),
            lax.all_gather(keyvalue[:, DK:], "seq", axis=0, tiled=True),
        ),
        jnp.int32(0),
    )
    attended = finish_attention(result, group_count)
    output_half = lax.dynamic_slice_in_dim(
        output_weight, col_index * local_heads * DV, local_heads * DV, 0
    )
    partial_out = jnp.dot(
        attended,
        lax.all_gather(output_half, "seq", axis=1, tiled=True),
        preferred_element_type=jnp.float32,
    )
    attention_out = lax.psum_scatter(
        partial_out.astype(jnp.bfloat16), "col", scatter_dimension=0, tiled=True
    ).astype(jnp.float32)
    tokens = (embedded.astype(jnp.float32) + attention_out).astype(jnp.bfloat16)
    pair_pool = jnp.mean(
        tokens.astype(jnp.float32).reshape(-1, PAIR_POOL, tokens.shape[1]), axis=1
    ).astype(jnp.bfloat16)
    projected = jnp.dot(pair_pool, rowcol_weight, preferred_element_type=jnp.float32).astype(
        jnp.bfloat16
    )
    features = pair_weight.shape[0]
    row_block = lax.all_gather(projected, "col", axis=0, tiled=True)
    column_all = lax.all_gather(row_block[:, features:], "seq", axis=0, tiled=True)
    row_part = row_block[:, :features]
    column_span = column_all.shape[0] // col_count
    column_part = lax.dynamic_slice_in_dim(
        column_all, lax.axis_index("col") * column_span, column_span, 0
    )
    hidden = jax.nn.gelu(
        row_part.astype(jnp.float32)[:, None, :] + column_part.astype(jnp.float32)[None, :, :],
        approximate=True,
    ).astype(jnp.bfloat16)
    pair_out = jnp.dot(
        hidden.reshape(-1, features), pair_weight, preferred_element_type=jnp.float32
    ).astype(jnp.bfloat16)
    return (tokens, pair_out.reshape(row_part.shape[0], column_span, features))


EDGE = 16
Y = 2
PIECES = (3, 1, 1, 1)
E, KV, Q, O = range(4)
PLAN = {
    "start": ((E,), (KV,),),
    "act": ((E, 1, 0),),
    "edges": ((E, 1, 1),),
    "mean": ((E, 1, 2),),
    "win": ((Q,), (KV, 1),),
    ("conv", 0): ((E, 2, 0),),
    ("conv", 1): ((E, 2, 1),),
    ("conv", 2): ((E, 2, 2), (KV, 2),),
    ("conv", 3): ((Q, 1), (O,),),
    "wait": ((E, 3, 0), (E, 3, 1), (E, 3, 2), (KV, 3),),
    ("swap", 0): ((Q, 2),),
    "kv": ((Q, 3), (O, 1),),
    "query": ((O, 2),),
    "kvz": ((O, 3),),
}


def fused_kernel(
    taps,
    heads,
    signal,
    conv_w,
    conv_gain,
    embed_w,
    attn_gain,
    query_w,
    kv_w,
    out_w,
    rowcol,
    pair_w,
    tokens_out,
    pair_out,
    sig,
    act,
    win,
    edge,
    halo,
    conv_buf,
    e_buf,
    q_buf,
    k_buf,
    o_buf,
    rc_buf,
    pools,
    part,
    other,
    emb,
    normed,
    ssq,
    scales,
    kv_part,
    q_part,
    kv_all,
    att,
    tok_peer,
    cols,
    rows_peer,
    gain_buf,
    hid,
    loc_sem,
    send_sem,
    recv_sem,
):
    f32, bf16 = jnp.float32, jnp.bfloat16
    n = lax.axis_size("seq")
    nz = n // Y
    s = lax.axis_index("seq")
    c = lax.axis_index("col")
    x = lax.axis_index("grp")
    z, y = s // Y, s % Y
    half = sig.shape[1]
    positions = sig.shape[2]
    count = positions // POOL
    width = e_buf.shape[1]
    halo_width = taps // 2
    started = []
    local = []

    def remote(src, dst, to):
        index = len(started)
        copy = pltpu.make_async_remote_copy(
            src_ref=src,
            dst_ref=dst,
            send_sem=send_sem.at[index],
            recv_sem=recv_sem.at[index],
            device_id=to,
            device_id_type=pl.DeviceIdType.MESH,
        )
        copy.start()
        started.append(copy)
        return copy

    def fetch(src, dst):
        copy = pltpu.make_async_copy(src, dst, loc_sem.at[len(local)])
        copy.start()
        local.append(copy)
        return copy

    def seq_of(z_index, y_index):
        return z_index * Y + y_index

    def z_from(dz):
        return (z + nz - dz) % nz

    def z_to(dz):
        return (z + dz) % nz

    partner = {"col": 1 - c}
    y_peer = {"seq": seq_of(z, 1 - y)}
    x_peer = {"grp": 1 - x}
    z_next = {"seq": seq_of(z_to(1), y)}

    sig_here = fetch(signal, sig.at[0])
    barrier = pltpu.get_barrier_semaphore()
    for d in range(n):
        for e in range(2):
            if d or e:
                pl.semaphore_signal(
                    barrier,
                    inc=1,
                    device_id={"seq": (s + d) % n, "col": (c + e) % 2},
                    device_id_type=pl.DeviceIdType.MESH,
                )
    pl.semaphore_signal(barrier, inc=1, device_id=x_peer, device_id_type=pl.DeviceIdType.MESH)

    k_rows = kv_w.shape[0] // 2
    q_cols = query_w.shape[1] // 2
    o_cols = out_w.shape[1] // 2
    kv_own = kv_w.at[pl.ds(pl.multiple_of(c * k_rows, 16), k_rows)]
    q_own = query_w.at[:, pl.ds(pl.multiple_of(c * q_cols, 128), q_cols)]
    o_own = out_w.at[:, pl.ds(pl.multiple_of(c * o_cols, 128), o_cols)]

    def k_at(owner):
        return k_buf.at[owner, pl.ds(pl.multiple_of(c * k_rows, 16), k_rows)]

    weights = [
        (embed_w, lambda owner: e_buf.at[owner]),
        (kv_own, k_at),
        (q_own, lambda owner: q_buf.at[owner]),
        (o_own, lambda owner: o_buf.at[owner]),
    ]
    conv_here = [fetch(conv_w.at[t], conv_buf.at[t]) for t in range(taps)]
    own_here = [fetch(own, at(z)) for own, at in weights]
    rc_here = []
    for k in range(nz):
        rows = pl.ds(pl.multiple_of(seq_of(k, y) * width, 16), width)
        rc_here.append(fetch(rowcol.at[rows], rc_buf.at[k]))

    row = lax.broadcasted_iota(jnp.int32, (EDGE, positions), 0)
    place = lax.broadcasted_iota(jnp.int32, (EDGE, positions), 1)
    wanted = jnp.where(row < EDGE // 2, row, row - EDGE // 2 + positions - halo_width)
    in_use = lax.rem(row, EDGE // 2) < halo_width
    pick = jnp.where((place == wanted) & in_use, 1.0, 0.0).astype(bf16)
    sig_here.wait()
    over_rows = (((1,), (1,)), ((), ()))
    edge[...] = lax.dot_general(pick, sig[0], over_rows, preferred_element_type=f32).astype(bf16)

    pl.semaphore_wait(barrier, 2 * n)

    signal_copy = remote(signal, sig.at[1], partner)
    copies = {}

    def piece(ref, w, p):
        rows = ref.shape[0] // 2 // PIECES[w]
        return ref.at[pl.ds(pl.multiple_of((x * PIECES[w] + p) * rows, 16), rows)]

    def begin(w, far=(1,)):
        own, at = weights[w]
        for p in range(PIECES[w]):
            for dz in far:
                to = {"seq": seq_of(z_to(dz), y)}
                copies[w, p, "z", dz] = remote(piece(own, w, p), piece(at(z), w, p), to)

    def hop(w, dz, p=None):
        _, at = weights[w]
        for p in range(PIECES[w]) if p is None else (p,):
            copies[w, p, "z", dz].wait_recv()
            ref = piece(at(z_from(dz)), w, p)
            if dz + 1 < nz and (w, p, "z", dz + 1) not in copies:
                copies[w, p, "z", dz + 1] = remote(ref, ref, z_next)
            copies[w, p, "x", dz] = remote(ref, ref, x_peer)

    def advance(point):
        for step in PLAN.get(point, ()):
            begin(step[0]) if len(step) == 1 else hop(*step)

    def arrived(w, dz):
        if dz == 0:
            own_here[w].wait()
        else:
            for p in range(PIECES[w]):
                copies[w, p, "x", dz].wait_recv()

    halo_copies = []
    for e in range(2):
        core = (c + e) % 2
        up = {"seq": (s + 1) % n, "col": core}
        down = {"seq": (s + n - 1) % n, "col": core}
        halo_copies.append(remote(edge, halo.at[e, 0], up))
        halo_copies.append(remote(edge, halo.at[e, 1], down))
    advance("start")

    def windows(position):
        column = lax.broadcasted_iota(jnp.int32, position.shape, 1)
        tap = column // count
        begin = (column - tap * count) * POOL + tap - halo_width
        hit = (position >= begin) & (position < begin + POOL)
        return jnp.where(hit, 1.0 / POOL, 0.0).astype(bf16)

    mean_of = windows(lax.broadcasted_iota(jnp.int32, (positions, taps * count), 0))
    edge_row = lax.broadcasted_iota(jnp.int32, (EDGE, taps * count), 0)
    edge_means = [windows(edge_row - EDGE // 2 - halo_width), windows(edge_row + positions)]
    edge_means = [
        jnp.where((edge_row >= EDGE // 2) & (s > 0), edge_means[0], 0.0).astype(bf16),
        jnp.where((edge_row < EDGE // 2) & (s < n - 1), edge_means[1], 0.0).astype(bf16),
    ]
    channels = 2 * half
    gain_row = conv_gain[...].reshape(1, channels)
    gains = [gain_row[:, :half], gain_row[:, half:]]
    gains = [jnp.where(c == h, gains[0], gains[1]) for h in range(2)]
    gain_columns = [jnp.broadcast_to(g, (128, half)).T for g in gains]

    signal_copy.wait_recv()

    block = 64
    square = jnp.zeros((1, positions), f32)
    for h in range(2):
        v = sig[h].astype(f32)
        square = square + jnp.sum(v * v, axis=0, keepdims=True)
    scale = lax.rsqrt(square * (1.0 / channels) + 1e-06)
    for h in range(2):
        for i in range(half // block):
            rows = slice(i * block, (i + 1) * block)
            v = sig[h, rows, :].astype(f32) * scale * gain_columns[h][rows, :1]
            act[h, rows, :] = jax.nn.gelu(v, approximate=True).astype(bf16)

    advance("act")
    for copy in halo_copies:
        copy.wait_recv()

    edges = [[], []]
    for side in range(2):
        a, b = halo[0, side].astype(f32), halo[1, side].astype(f32)
        square = jnp.sum(a * a, axis=1, keepdims=True) + jnp.sum(b * b, axis=1, keepdims=True)
        edge_scale = lax.rsqrt(square * (1.0 / channels) + 1e-06)
        for h, v in enumerate((a, b)):
            v = jax.nn.gelu(v * edge_scale * gains[h], approximate=True)
            edges[h].append(v.T.astype(bf16))
    advance("edges")
    for h in range(2):
        if h:
            advance("mean")
        core = c if h == 0 else 1 - c
        mean = jnp.dot(act[h], mean_of, preferred_element_type=f32)
        for side in range(2):
            mean = mean + jnp.dot(edges[h][side], edge_means[side], preferred_element_type=f32)
        win[pl.ds(pl.multiple_of(core * half, 16), half), :] = mean.astype(bf16)

    advance("win")

    middle = slice(halo_width * count, (halo_width + 1) * count)
    for copy in conv_here:
        copy.wait()
    chunks = 4
    size = half // chunks
    pool_copies = []
    for i in range(chunks):
        rows = slice(i * size, (i + 1) * size)
        total = jnp.dot(sig[0, rows, :], mean_of[:, middle], preferred_element_type=f32)
        for t in range(taps):
            total = total + jnp.dot(
                conv_buf[t, rows, :],
                win[:, t * count : (t + 1) * count],
                preferred_element_type=f32,
            )
        pools[0, rows, :] = total.astype(bf16)
        span = pl.ds(i * size, size)
        pool_copies.append(remote(pools.at[0, span], pools.at[1, span], y_peer))
        advance(("conv", i))

    gain_row = attn_gain[...].reshape(1, n * width)
    for k in range(n):
        gain_buf[k] = gain_row[:, k * width : (k + 1) * width]
    own_half = pl.ds(pl.multiple_of(c * (count // 2), 16), count // 2)
    peer_half = pl.ds(pl.multiple_of(count + c * (count // 2), 16), count // 2)
    advance("wait")
    for copy in pool_copies:
        copy.wait_recv()
    both = jnp.concatenate([pools[0], pools[1]], axis=1)
    square = jnp.zeros((1, 2 * count), f32)
    kv = 0.0
    for k in range(0, nz, 2):
        order = (k, k + 1)
        owners = [z_from(dz) for dz in order]
        swaps = []
        for dz, owner in zip(order, owners):
            advance(("owner", dz))
            arrived(E, dz)
            part[0, owner] = jnp.dot(e_buf[owner], both, preferred_element_type=f32).astype(bf16)
            swaps.append(remote(part.at[0, owner], other.at[0, owner], partner))
        for dz, owner in zip(order, owners):
            advance(("pass", dz))
            arrived(KV, dz)
            ref = k_at(owner)
            swaps.append(remote(ref, ref, partner))
        for copy in swaps[:2]:
            copy.wait_recv()
        advance(("swap", k))
        pair = []
        for owner in owners:
            v = (part[0, owner].astype(f32) + other[0, owner].astype(f32)).astype(bf16)
            emb[owner] = v
            v = v.astype(f32)
            square = square + jnp.sum(v * v, axis=0, keepdims=True)
            pair.append(v)
        gain = jnp.concatenate([gain_buf[seq_of(owner, y)] for owner in owners], axis=1)
        columns = slice(k * width, (k + 2) * width)
        normed[:, columns] = (jnp.concatenate(pair, axis=0).T * gain).astype(bf16)
        for copy in swaps[2:]:
            copy.wait_recv()
        kv = kv + jnp.dot(
            jnp.concatenate([normed[own_half, columns], normed[peer_half, columns]], axis=0),
            jnp.concatenate([k_buf[owner] for owner in owners], axis=0),
            preferred_element_type=f32,
        )
    kv_part[0] = kv[count // 2 :].astype(bf16)
    kv_swap = remote(kv_part.at[0], kv_part.at[1], y_peer)
    ssq[0] = jnp.broadcast_to(square[:, count:], (8, count))
    ssq_copy = remote(ssq.at[0], ssq.at[1], y_peer)

    advance("kv")
    ssq_copy.wait_recv()
    square = square[:, :count] + ssq[1, 0:1, :]
    scale = lax.rsqrt(square * (1.0 / (n * width)) + 1e-06)
    scales[...] = jnp.broadcast_to(scale, (128, count)).T

    def kv_at(owner):
        return kv_all.at[owner, own_half]

    kv_swap.wait_recv()
    kv = (kv[: count // 2] + kv_part[1].astype(f32)) * scales[own_half, :1]
    kv_all[s, own_half, :] = kv.astype(bf16)
    mine = kv_at(s)
    kv_copies = {}
    for dz in (2, 1, 3):
        kv_copies["z", dz] = remote(mine, mine, {"seq": seq_of(z_to(dz), y)})
    kv_copies["y", 0] = remote(mine, mine, y_peer)
    across = [remote(mine, mine, partner)]
    advance("sent")
    for dz in range(nz):
        arrived(Q, dz)
    queries = jnp.dot(
        normed[...],
        jnp.concatenate([q_buf[z_from(dz)] for dz in range(nz)], axis=0),
        preferred_element_type=f32,
    )
    q_part[0] = queries[count:].astype(bf16)
    q_swap = remote(q_part.at[0], q_part.at[1], y_peer)

    advance("query")
    q_swap.wait_recv()
    queries = (queries[:count] + q_part[1].astype(f32)) * (scales[:, :1] * (DK**-0.5))
    queries = queries.astype(bf16)
    advance("scaled")
    for dz in (1, 3, 2):
        kv_copies["z", dz].wait_recv()
        ref = kv_at(seq_of(z_from(dz), y))
        kv_copies["y", dz] = remote(ref, ref, y_peer)
        across.append(remote(ref, ref, partner))
    advance("kvz")
    for dz in (0, 1, 3, 2):
        kv_copies["y", dz].wait_recv()
        ref = kv_at(seq_of(z_from(dz), 1 - y))
        across.append(remote(ref, ref, partner))
    advance("kvy")
    for copy in across:
        copy.wait_recv()

    everything = kv_all[...].reshape(n * count, kv_all.shape[2])
    keys, values = everything[:, :DK], everything[:, DK:]
    att_copies = []
    for h in range(0, heads, 2):
        mixes = []
        for i in (h, h + 1):
            scores = lax.dot_general(
                queries[:, i * DK : (i + 1) * DK],
                keys,
                over_rows,
                preferred_element_type=f32,
            )
            exps = jnp.exp(scores - jnp.max(scores, axis=1, keepdims=True))
            norm = jnp.sum(exps, axis=1, keepdims=True)
            mixed = jnp.dot(exps.astype(bf16), values, preferred_element_type=f32)
            mixes.append((mixed / norm).astype(bf16))
        att[0, :, h * DV : (h + 2) * DV] = jnp.concatenate(mixes, axis=1)
        span = pl.ds(h * DV, 2 * DV)
        att_copies.append(remote(att.at[0, :, span], att.at[1, :, span], y_peer))

    advance("mixed")
    for dz in range(nz):
        arrived(O, dz)
    rows_n = count // PAIR_POOL
    features = pair_w.shape[0]
    token_copies = []
    for j in range(Y):
        if j:
            advance("out")
        span = slice(j * count, (j + 1) * count)
        there = pl.ds(j * count, count)
        swaps = []
        for k in range(0, nz, 2):
            acc = 0.0
            for h in range(0, heads, 2):
                if j and not k:
                    att_copies[h // 2].wait_recv()
                across_heads = slice(h * DV, (h + 2) * DV)
                acc = acc + lax.dot_general(
                    o_buf[k : k + 2, :, across_heads].reshape(2 * width, 2 * DV),
                    att[j, :, across_heads],
                    over_rows,
                    preferred_element_type=f32,
                )
            part[1, k : k + 2, :, span] = acc.reshape(2, width, count).astype(bf16)
            both = pl.ds(k, 2)
            swaps.append(
                remote(part.at[1, both, :, there], other.at[1, both, :, there], partner)
            )
        for k in range(0, nz, 2):
            swaps[k // 2].wait_recv()
            columns = slice(k * width, (k + 2) * width)
            pair = [
                emb[b, :, span].astype(f32)
                + (part[1, b, :, span].astype(f32) + other[1, b, :, span].astype(f32))
                for b in (k, k + 1)
            ]
            normed[span, columns] = jnp.concatenate(pair, axis=0).T.astype(bf16)
            if j:
                there = pl.ds(k * width, 2 * width)
                token_copies.append(
                    remote(normed.at[peer_half, there], tok_peer.at[:, there], y_peer)
                )
    row_of = lax.broadcasted_iota(jnp.int32, (2 * rows_n, 2 * count), 0)
    token_of = lax.broadcasted_iota(jnp.int32, (2 * rows_n, 2 * count), 1) // PAIR_POOL
    pool = jnp.where(row_of == token_of, 1.0 / PAIR_POOL, 0.0).astype(bf16)
    for copy in rc_here:
        copy.wait()
    pair_pool = jnp.dot(pool, normed[...], preferred_element_type=f32).astype(bf16)
    projected = jnp.dot(
        pair_pool, rc_buf[...].reshape(nz * width, 2 * features), preferred_element_type=f32
    )
    cols[s] = projected[:, features:].astype(bf16)
    rows_peer[0] = projected[:, :features].astype(bf16)
    rows_copy = remote(rows_peer.at[0], rows_peer.at[1], y_peer)
    col_copies = []
    for d in range(1, n):
        to = {"seq": (s + d) % n}
        col_copies.append(remote(cols.at[s], cols.at[s], to))
    rows_copy.wait_recv()
    row_part = projected[:rows_n, :features] + rows_peer[1].astype(f32)[rows_n:]
    row_part = row_part.astype(bf16).astype(f32)[:, None, :]
    for copy in token_copies:
        copy.wait_recv()
    tok_own, tok_other = normed[own_half, :], tok_peer[...]
    for k in range(nz):
        a = tok_own[:, k * width : (k + 1) * width]
        b = tok_other[:, k * width : (k + 1) * width]
        pair = [jnp.where(y == 0, a, b), jnp.where(y == 0, b, a)]
        tokens_out[:, k * 2 * width : (k + 1) * 2 * width] = jnp.concatenate(pair, axis=1)
    for copy in col_copies:
        copy.wait_recv()
    for j in range(nz // 2):
        both = [cols[c * (n // 2) + Y * j + i].astype(f32) for i in range(Y)]
        for i in range(Y):
            column = both[i][:rows_n] + both[1 - i][rows_n:]
            column = column.astype(bf16).astype(f32)
            hid[:, pl.ds((Y * j + i) * rows_n, rows_n), :] = jax.nn.gelu(
                row_part + column[None, :, :], approximate=True
            )
    hidden = hid[...].reshape(rows_n * (n // 2) * rows_n, features).astype(bf16)
    result = jnp.dot(hidden, pair_w[...], preferred_element_type=f32)
    pair_out[...] = result.reshape(pair_out.shape).astype(bf16)
    for copy in started:
        copy.wait_send()


def hand_over(tokens, pair, tokens_out, pair_out):
    tokens_out[...] = tokens[...]
    pair_out[...] = pair[...]


def on_device_fused(
    signal,
    conv_weight,
    conv_gain,
    embed_weight,
    attn_gain,
    query_weight,
    keyvalue_weight,
    output_weight,
    rowcol_weight,
    pair_weight,
):
    bf16, f32 = jnp.bfloat16, jnp.float32
    n = lax.axis_size("seq")
    nz = n // Y
    positions, half = signal.shape
    taps, channels, _ = conv_weight.shape
    count = positions // POOL
    width = embed_weight.shape[1]
    q_cols = query_weight.shape[1] // 2
    heads = q_cols // DK
    kv_cols = keyvalue_weight.shape[1]
    rows_n = count // PAIR_POOL
    features = pair_weight.shape[0]
    any_spec = pl.BlockSpec(memory_space=pl.ANY)
    vmem = pl.BlockSpec(memory_space=pltpu.VMEM)
    dma = pltpu.SemaphoreType.DMA
    tokens, pair = pl.pallas_call(
        functools.partial(fused_kernel, taps, heads),
        out_shape=(
            jax.ShapeDtypeStruct((count // 2, n * width), bf16),
            jax.ShapeDtypeStruct((rows_n, rows_n * n // 2, features), bf16),
        ),
        in_specs=[any_spec, any_spec, vmem, any_spec, vmem]
        + [any_spec, any_spec, any_spec, any_spec, vmem],
        out_specs=(vmem, vmem),
        scratch_shapes=[
            pltpu.VMEM((2, half, positions), bf16),
            pltpu.VMEM((2, half, positions), bf16),
            pltpu.VMEM((2 * half, taps * count), bf16),
            pltpu.VMEM((EDGE, half), bf16),
            pltpu.VMEM((2, 2, EDGE, half), bf16),
            pltpu.VMEM((taps, half, channels), bf16),
            pltpu.VMEM((nz, width, half), bf16),
            pltpu.VMEM((nz, width, q_cols), bf16),
            pltpu.VMEM((nz, width, kv_cols), bf16),
            pltpu.VMEM((nz, width, heads * DV), bf16),
            pltpu.VMEM((nz, width, 2 * features), bf16),
            pltpu.VMEM((2, half, count), bf16),
            pltpu.VMEM((2, nz, width, 2 * count), bf16),
            pltpu.VMEM((2, nz, width, 2 * count), bf16),
            pltpu.VMEM((nz, width, 2 * count), bf16),
            pltpu.VMEM((2 * count, nz * width), bf16),
            pltpu.VMEM((2, 8, count), f32),
            pltpu.VMEM((count, 128), f32),
            pltpu.VMEM((2, count // 2, kv_cols), bf16),
            pltpu.VMEM((2, count, q_cols), bf16),
            pltpu.VMEM((n, count, kv_cols), bf16),
            pltpu.VMEM((2, count, heads * DV), bf16),
            pltpu.VMEM((count // 2, nz * width), bf16),
            pltpu.VMEM((n, 2 * rows_n, features), bf16),
            pltpu.VMEM((2, 2 * rows_n, features), bf16),
            pltpu.VMEM((n, 1, width), f32),
            pltpu.VMEM((rows_n, rows_n * n // 2, features), f32),
            dma((32,)),
            dma((160,)),
            dma((160,)),
        ],
        compiler_params=pltpu.CompilerParams(
            collective_id=0, has_side_effects=True, vmem_limit_bytes=60 * 1024 * 1024
        ),
    )(
        signal.T,
        jnp.swapaxes(conv_weight, 1, 2),
        conv_gain,
        embed_weight.T,
        attn_gain,
        query_weight,
        keyvalue_weight,
        output_weight.T,
        rowcol_weight,
        pair_weight,
    )
    return pl.pallas_call(
        hand_over,
        out_shape=(
            jax.ShapeDtypeStruct(tokens.shape, bf16),
            jax.ShapeDtypeStruct(pair.shape, bf16),
        ),
        in_specs=[vmem, vmem],
        out_specs=(vmem, vmem),
    )(tokens, pair)


def fits(mesh):
    n = mesh.shape["seq"]
    return n == 8 and mesh.shape["col"] == 2 and mesh.shape["grp"] == 2


def solution(mesh):
    placed = (
        P(("grp", "seq"), "col"),
        P(None, None, "col"),
        P(),
        P("col", "seq"),
        P(),
        P("seq", None),
        P("seq", None),
        P(None, "seq"),
        P(),
        P(),
    )
    return jax.shard_map(
        on_device_fused if fits(mesh) else on_device,
        mesh=mesh,
        in_specs=placed,
        out_specs=(P(("grp", "seq", "col"), None), P(("grp", "seq"), "col", None)),
        check_vma=False,
    )
```

```python
import functools

import jax
import jax.numpy as jnp
from jax import lax
from jax.experimental import pallas as pl
from jax.experimental.pallas import tpu as pltpu
from jax.sharding import PartitionSpec as P

DK = 128
DV = 192
POOL = 4
PAIR_POOL = 16


def with_halo(array, sides, width):
    for axis, dim in sides:
        size, length = (lax.axis_size(axis), array.shape[dim])
        up = [(i, (i + 1) % size) for i in range(size - 1)]
        down = [(j, i) for i, j in up]
        last = lax.slice_in_dim(array, length - width, length, axis=dim)
        first = lax.slice_in_dim(array, 0, width, axis=dim)
        before = lax.ppermute(last, axis, up)
        after = lax.ppermute(first, axis, down)
        array = jnp.concatenate([before, array, after], axis=dim)
    return array


def rms_scale(values, gain_vector):
    return (
        values * lax.rsqrt(jnp.mean(values * values, axis=-1, keepdims=True) + 1e-06) * gain_vector
    )


def attention_parts(queries, head_count):
    query_rows = queries.reshape(queries.shape[0] * head_count, DK)

    def absorb(running, pieces, first_row):
        running_max, running_sum, accumulated = running
        key_piece, value_piece = pieces
        scores = lax.dot_general(
            query_rows, key_piece, (((1,), (1,)), ((), ())), preferred_element_type=jnp.float32
        )
        newest_max = jnp.maximum(running_max, jnp.max(scores, axis=1))
        weights = jnp.exp(scores - newest_max[:, None])
        running_sum = jnp.sum(weights, axis=1)
        accumulated = jnp.dot(
            weights.astype(jnp.bfloat16), value_piece, preferred_element_type=jnp.float32
        )
        return (newest_max, running_sum, accumulated)

    row_count = query_rows.shape[0]
    initial = (
        jnp.full((row_count,), -1e30, jnp.float32),
        jnp.zeros((row_count,), jnp.float32),
        jnp.zeros((row_count, DV), jnp.float32),
    )
    return (absorb, initial)


def finish_attention(result, token_count):
    running_max, running_sum, accumulated = result
    return (accumulated / running_sum[:, None]).astype(jnp.bfloat16).reshape(token_count, -1)


def on_device(
    signal,
    conv_weight,
    conv_gain,
    embed_weight,
    attn_gain,
    query_weight,
    keyvalue_weight,
    output_weight,
    rowcol_weight,
    pair_weight,
):
    positions = signal.shape[0]
    tap_count = conv_weight.shape[0]
    halo_width = tap_count // 2
    padded = with_halo(signal, (("seq", 0),), halo_width)
    widened = lax.all_gather(padded, "col", axis=1, tiled=True)
    activated = jax.nn.gelu(
        rms_scale(widened.astype(jnp.float32), conv_gain), approximate=True
    ).astype(jnp.bfloat16)
    summed = signal.astype(jnp.float32)
    for tap_index in range(tap_count):
        summed = summed + jnp.dot(
            activated[tap_index : tap_index + positions],
            conv_weight[tap_index],
            preferred_element_type=jnp.float32,
        )
    pooled = jnp.mean(summed.reshape(positions // POOL, POOL, -1), axis=1).astype(jnp.bfloat16)
    embed_full = lax.all_gather(embed_weight, "seq", axis=1, tiled=True)
    col_count = lax.axis_size("col")
    embedded = lax.psum_scatter(
        jnp.dot(pooled, embed_full, preferred_element_type=jnp.float32).astype(jnp.bfloat16),
        "col",
        scatter_dimension=0,
        tiled=True,
    )
    normed = rms_scale(embedded.astype(jnp.float32), attn_gain).astype(jnp.bfloat16)
    head_count = query_weight.shape[1] // DK
    scaling = DK ** (-0.5)
    col_index = lax.axis_index("col")
    local_heads = head_count // col_count
    group_tokens = lax.all_gather(normed, "col", axis=0, tiled=True)
    group_count = group_tokens.shape[0]
    query_half = lax.dynamic_slice_in_dim(
        query_weight, col_index * local_heads * DK, local_heads * DK, 1
    )
    query_sum = jnp.dot(
        group_tokens,
        lax.all_gather(query_half, "seq", axis=0, tiled=True),
        preferred_element_type=jnp.float32,
    )
    keyvalue_sum = jnp.dot(
        group_tokens,
        lax.all_gather(keyvalue_weight, "seq", axis=0, tiled=True),
        preferred_element_type=jnp.float32,
    )
    queries = (query_sum * scaling).astype(jnp.bfloat16)
    keyvalue = keyvalue_sum.astype(jnp.bfloat16)
    absorb, initial = attention_parts(queries, local_heads)
    result = absorb(
        initial,
        (
            lax.all_gather(keyvalue[:, :DK], "seq", axis=0, tiled=True),
            lax.all_gather(keyvalue[:, DK:], "seq", axis=0, tiled=True),
        ),
        jnp.int32(0),
    )
    attended = finish_attention(result, group_count)
    output_half = lax.dynamic_slice_in_dim(
        output_weight, col_index * local_heads * DV, local_heads * DV, 0
    )
    partial_out = jnp.dot(
        attended,
        lax.all_gather(output_half, "seq", axis=1, tiled=True),
        preferred_element_type=jnp.float32,
    )
    attention_out = lax.psum_scatter(
        partial_out.astype(jnp.bfloat16), "col", scatter_dimension=0, tiled=True
    ).astype(jnp.float32)
    tokens = (embedded.astype(jnp.float32) + attention_out).astype(jnp.bfloat16)
    pair_pool = jnp.mean(
        tokens.astype(jnp.float32).reshape(-1, PAIR_POOL, tokens.shape[1]), axis=1
    ).astype(jnp.bfloat16)
    projected = jnp.dot(pair_pool, rowcol_weight, preferred_element_type=jnp.float32).astype(
        jnp.bfloat16
    )
    features = pair_weight.shape[0]
    row_block = lax.all_gather(projected, "col", axis=0, tiled=True)
    column_all = lax.all_gather(row_block[:, features:], "seq", axis=0, tiled=True)
    row_part = row_block[:, :features]
    column_span = column_all.shape[0] // col_count
    column_part = lax.dynamic_slice_in_dim(
        column_all, lax.axis_index("col") * column_span, column_span, 0
    )
    hidden = jax.nn.gelu(
        row_part.astype(jnp.float32)[:, None, :] + column_part.astype(jnp.float32)[None, :, :],
        approximate=True,
    ).astype(jnp.bfloat16)
    pair_out = jnp.dot(
        hidden.reshape(-1, features), pair_weight, preferred_element_type=jnp.float32
    ).astype(jnp.bfloat16)
    return (tokens, pair_out.reshape(row_part.shape[0], column_span, features))


EDGE = 16
Y = 2
PIECES = (3, 1, 2, 2)
E, KV, Q, O = range(4)
ORDER = (0, 1, 3, 2)
PLAN = {
    "start": ((E,), (KV,),),
    "act": ((E, 1, 0),),
    "edges": ((E, 1, 1),),
    "mean": ((E, 1, 2), (E, 3, 0),),
    "win": ((E, 3, 1), (E, 3, 2), (KV, 1), (Q,),),
    ("conv", 1): ((E, 2, 0),),
    ("conv", 2): ((E, 2, 1), (KV, 3),),
    "wait": ((E, 2, 2), (KV, 2), (Q, 1),),
    ("pass", 0): ((O,),),
    ("swap", 0): ((Q, 3),),
    ("swap", 2): ((Q, 2),),
    "kv": ((O, 1), (O, 3),),
    "query": ((O, 2),),
}


def fused_kernel(
    taps,
    heads,
    signal,
    conv_w,
    conv_gain,
    embed_w,
    attn_gain,
    query_w,
    kv_w,
    out_w,
    rowcol,
    pair_w,
    tokens_out,
    pair_out,
    sig,
    act,
    win,
    edge,
    halo,
    conv_buf,
    e_buf,
    q_buf,
    k_buf,
    o_buf,
    rc_buf,
    pools,
    part,
    other,
    emb,
    normed,
    ssq,
    scales,
    kv_part,
    q_part,
    kv_all,
    att,
    tok_peer,
    cols,
    rows_peer,
    gain_buf,
    hid,
    loc_sem,
    send_sem,
    recv_sem,
):
    f32, bf16 = jnp.float32, jnp.bfloat16
    n = lax.axis_size("seq")
    nz = n // Y
    s = lax.axis_index("seq")
    c = lax.axis_index("col")
    x = lax.axis_index("grp")
    z, y = s // Y, s % Y
    half = sig.shape[1]
    positions = sig.shape[2]
    count = positions // POOL
    width = e_buf.shape[1]
    halo_width = taps // 2
    started = []
    local = []

    def remote(src, dst, to):
        index = len(started)
        copy = pltpu.make_async_remote_copy(
            src_ref=src,
            dst_ref=dst,
            send_sem=send_sem.at[index],
            recv_sem=recv_sem.at[index],
            device_id=to,
            device_id_type=pl.DeviceIdType.MESH,
        )
        copy.start()
        started.append(copy)
        return copy

    def fetch(src, dst):
        copy = pltpu.make_async_copy(src, dst, loc_sem.at[len(local)])
        copy.start()
        local.append(copy)
        return copy

    def seq_of(z_index, y_index):
        return z_index * Y + y_index

    def z_from(dz):
        return (z + nz - dz) % nz

    def z_to(dz):
        return (z + dz) % nz

    partner = {"col": 1 - c}
    y_peer = {"seq": seq_of(z, 1 - y)}
    x_peer = {"grp": 1 - x}
    z_next = {"seq": seq_of(z_to(1), y)}

    sig_here = fetch(signal, sig.at[0])
    barrier = pltpu.get_barrier_semaphore()
    for d in range(n):
        for e in range(2):
            if d or e:
                pl.semaphore_signal(
                    barrier,
                    inc=1,
                    device_id={"seq": (s + d) % n, "col": (c + e) % 2},
                    device_id_type=pl.DeviceIdType.MESH,
                )
    pl.semaphore_signal(barrier, inc=1, device_id=x_peer, device_id_type=pl.DeviceIdType.MESH)

    k_rows = kv_w.shape[0] // 2
    q_cols = query_w.shape[1] // 2
    o_cols = out_w.shape[1] // 2
    kv_own = kv_w.at[pl.ds(pl.multiple_of(c * k_rows, 16), k_rows)]
    q_own = query_w.at[:, pl.ds(pl.multiple_of(c * q_cols, 128), q_cols)]
    o_own = out_w.at[:, pl.ds(pl.multiple_of(c * o_cols, 128), o_cols)]

    def k_at(owner):
        return k_buf.at[owner, pl.ds(pl.multiple_of(c * k_rows, 16), k_rows)]

    weights = [
        (embed_w, lambda owner: e_buf.at[owner]),
        (kv_own, k_at),
        (q_own, lambda owner: q_buf.at[owner]),
        (o_own, lambda owner: o_buf.at[owner]),
    ]
    conv_here = [fetch(conv_w.at[t], conv_buf.at[t]) for t in range(taps)]
    own_here = [fetch(own, at(z)) for own, at in weights]
    rc_here = []
    for k in range(nz):
        rows = pl.ds(pl.multiple_of(seq_of(k, y) * width, 16), width)
        rc_here.append(fetch(rowcol.at[rows], rc_buf.at[k]))

    row = lax.broadcasted_iota(jnp.int32, (EDGE, positions), 0)
    place = lax.broadcasted_iota(jnp.int32, (EDGE, positions), 1)
    wanted = jnp.where(row < EDGE // 2, row, row - EDGE // 2 + positions - halo_width)
    in_use = lax.rem(row, EDGE // 2) < halo_width
    pick = jnp.where((place == wanted) & in_use, 1.0, 0.0).astype(bf16)
    sig_here.wait()
    over_rows = (((1,), (1,)), ((), ()))
    edge[...] = lax.dot_general(pick, sig[0], over_rows, preferred_element_type=f32).astype(bf16)

    pl.semaphore_wait(barrier, 2 * n)

    signal_copy = remote(signal, sig.at[1], partner)
    copies = {}

    def piece(ref, w, p):
        rows = ref.shape[0] // 2 // PIECES[w]
        return ref.at[pl.ds(pl.multiple_of((x * PIECES[w] + p) * rows, 16), rows)]

    def begin(w, far=(1, 3)):
        own, at = weights[w]
        for p in range(PIECES[w]):
            for dz in far:
                to = {"seq": seq_of(z_to(dz), y)}
                copies[w, p, "z", dz] = remote(piece(own, w, p), piece(at(z), w, p), to)

    def hop(w, dz, p=None):
        _, at = weights[w]
        for p in range(PIECES[w]) if p is None else (p,):
            copies[w, p, "z", dz].wait_recv()
            ref = piece(at(z_from(dz)), w, p)
            if dz + 1 < nz and (w, p, "z", dz + 1) not in copies:
                copies[w, p, "z", dz + 1] = remote(ref, ref, z_next)
            copies[w, p, "x", dz] = remote(ref, ref, x_peer)

    def advance(point):
        for step in PLAN.get(point, ()):
            begin(step[0]) if len(step) == 1 else hop(*step)

    def arrived(w, dz):
        if dz == 0:
            own_here[w].wait()
        else:
            for p in range(PIECES[w]):
                copies[w, p, "x", dz].wait_recv()

    halo_copies = []
    for e in range(2):
        core = (c + e) % 2
        up = {"seq": (s + 1) % n, "col": core}
        down = {"seq": (s + n - 1) % n, "col": core}
        halo_copies.append(remote(edge, halo.at[e, 0], up))
        halo_copies.append(remote(edge, halo.at[e, 1], down))
    advance("start")

    def windows(position):
        column = lax.broadcasted_iota(jnp.int32, position.shape, 1)
        tap = column // count
        begin = (column - tap * count) * POOL + tap - halo_width
        hit = (position >= begin) & (position < begin + POOL)
        return jnp.where(hit, 1.0 / POOL, 0.0).astype(bf16)

    mean_of = windows(lax.broadcasted_iota(jnp.int32, (positions, taps * count), 0))
    edge_row = lax.broadcasted_iota(jnp.int32, (EDGE, taps * count), 0)
    edge_means = [windows(edge_row - EDGE // 2 - halo_width), windows(edge_row + positions)]
    edge_means = [
        jnp.where((edge_row >= EDGE // 2) & (s > 0), edge_means[0], 0.0).astype(bf16),
        jnp.where((edge_row < EDGE // 2) & (s < n - 1), edge_means[1], 0.0).astype(bf16),
    ]
    channels = 2 * half
    gain_row = conv_gain[...].reshape(1, channels)
    gains = [gain_row[:, :half], gain_row[:, half:]]
    gains = [jnp.where(c == h, gains[0], gains[1]) for h in range(2)]
    gain_columns = [jnp.broadcast_to(g, (128, half)).T for g in gains]

    signal_copy.wait_recv()

    block = 64
    square = jnp.zeros((1, positions), f32)
    for h in range(2):
        v = sig[h].astype(f32)
        square = square + jnp.sum(v * v, axis=0, keepdims=True)
    scale = lax.rsqrt(square * (1.0 / channels) + 1e-06)
    for h in range(2):
        if h:
            advance("half")
        for i in range(half // block):
            rows = slice(i * block, (i + 1) * block)
            v = sig[h, rows, :].astype(f32) * scale * gain_columns[h][rows, :1]
            act[h, rows, :] = jax.nn.gelu(v, approximate=True).astype(bf16)

    advance("act")
    for copy in halo_copies:
        copy.wait_recv()

    edges = [[], []]
    for side in range(2):
        a, b = halo[0, side].astype(f32), halo[1, side].astype(f32)
        square = jnp.sum(a * a, axis=1, keepdims=True) + jnp.sum(b * b, axis=1, keepdims=True)
        edge_scale = lax.rsqrt(square * (1.0 / channels) + 1e-06)
        for h, v in enumerate((a, b)):
            v = jax.nn.gelu(v * edge_scale * gains[h], approximate=True)
            edges[h].append(v.T.astype(bf16))
    advance("edges")
    for h in range(2):
        if h:
            advance("mean")
        core = c if h == 0 else 1 - c
        mean = jnp.dot(act[h], mean_of, preferred_element_type=f32)
        for side in range(2):
            mean = mean + jnp.dot(edges[h][side], edge_means[side], preferred_element_type=f32)
        win[pl.ds(pl.multiple_of(core * half, 16), half), :] = mean.astype(bf16)

    advance("win")

    middle = slice(halo_width * count, (halo_width + 1) * count)
    for copy in conv_here:
        copy.wait()
    chunks = 4
    size = half // chunks
    pool_copies = []
    for i in range(chunks):
        rows = slice(i * size, (i + 1) * size)
        total = jnp.dot(sig[0, rows, :], mean_of[:, middle], preferred_element_type=f32)
        for t in range(taps):
            if t == halo_width:
                advance(("tap", i))
            total = total + jnp.dot(
                conv_buf[t, rows, :],
                win[:, t * count : (t + 1) * count],
                preferred_element_type=f32,
            )
        pools[0, rows, :] = total.astype(bf16)
        span = pl.ds(i * size, size)
        pool_copies.append(remote(pools.at[0, span], pools.at[1, span], y_peer))
        advance(("conv", i))

    gain_row = attn_gain[...].reshape(1, n * width)
    for k in range(n):
        gain_buf[k] = gain_row[:, k * width : (k + 1) * width]
    own_half = pl.ds(pl.multiple_of(c * (count // 2), 16), count // 2)
    peer_half = pl.ds(pl.multiple_of(count + c * (count // 2), 16), count // 2)
    advance("wait")
    for copy in pool_copies:
        copy.wait_recv()
    both = jnp.concatenate([pools[0], pools[1]], axis=1)
    square = jnp.zeros((1, 2 * count), f32)
    kv = 0.0
    for k in range(0, nz, 2):
        order = ORDER[k : k + 2]
        owners = [z_from(dz) for dz in order]
        swaps = []
        for dz, owner in zip(order, owners):
            advance(("owner", dz))
            arrived(E, dz)
            part[0, owner] = jnp.dot(e_buf[owner], both, preferred_element_type=f32).astype(bf16)
            swaps.append(remote(part.at[0, owner], other.at[0, owner], partner))
        for dz, owner in zip(order, owners):
            advance(("pass", dz))
            arrived(KV, dz)
            ref = k_at(owner)
            swaps.append(remote(ref, ref, partner))
        for copy in swaps[:2]:
            copy.wait_recv()
        advance(("swap", k))
        pair = []
        for owner in owners:
            v = (part[0, owner].astype(f32) + other[0, owner].astype(f32)).astype(bf16)
            emb[owner] = v
            v = v.astype(f32)
            square = square + jnp.sum(v * v, axis=0, keepdims=True)
            pair.append(v)
        gain = jnp.concatenate([gain_buf[seq_of(owner, y)] for owner in owners], axis=1)
        columns = slice(k * width, (k + 2) * width)
        normed[:, columns] = (jnp.concatenate(pair, axis=0).T * gain).astype(bf16)
        for copy in swaps[2:]:
            copy.wait_recv()
        kv = kv + jnp.dot(
            jnp.concatenate([normed[own_half, columns], normed[peer_half, columns]], axis=0),
            jnp.concatenate([k_buf[owner] for owner in owners], axis=0),
            preferred_element_type=f32,
        )
    kv_part[0] = kv[count // 2 :].astype(bf16)
    kv_swap = remote(kv_part.at[0], kv_part.at[1], y_peer)
    ssq[0] = jnp.broadcast_to(square[:, count:], (8, count))
    ssq_copy = remote(ssq.at[0], ssq.at[1], y_peer)

    advance("kv")
    ssq_copy.wait_recv()
    square = square[:, :count] + ssq[1, 0:1, :]
    scale = lax.rsqrt(square * (1.0 / (n * width)) + 1e-06)
    scales[...] = jnp.broadcast_to(scale, (128, count)).T

    def kv_at(owner):
        return kv_all.at[owner, own_half]

    kv_swap.wait_recv()
    kv = (kv[: count // 2] + kv_part[1].astype(f32)) * scales[own_half, :1]
    kv_all[s, own_half, :] = kv.astype(bf16)
    mine = kv_at(s)
    kv_copies = {}
    for dz in (2, 1, 3):
        kv_copies["z", dz] = remote(mine, mine, {"seq": seq_of(z_to(dz), y)})
    kv_copies["y", 0] = remote(mine, mine, y_peer)
    across = [remote(mine, mine, partner)]
    advance("sent")
    for dz in range(nz):
        arrived(Q, dz)
    queries = jnp.dot(
        normed[...],
        jnp.concatenate([q_buf[z_from(dz)] for dz in ORDER], axis=0),
        preferred_element_type=f32,
    )
    q_part[0] = queries[count:].astype(bf16)
    q_swap = remote(q_part.at[0], q_part.at[1], y_peer)

    advance("query")
    q_swap.wait_recv()
    queries = (queries[:count] + q_part[1].astype(f32)) * (scales[:, :1] * (DK**-0.5))
    queries = queries.astype(bf16)
    for dz in (1, 3, 2):
        advance(("z", dz))
        kv_copies["z", dz].wait_recv()
        ref = kv_at(seq_of(z_from(dz), y))
        kv_copies["y", dz] = remote(ref, ref, y_peer)
        across.append(remote(ref, ref, partner))
    for dz in (0, 1, 3, 2):
        advance(("y", dz))
        kv_copies["y", dz].wait_recv()
        ref = kv_at(seq_of(z_from(dz), 1 - y))
        across.append(remote(ref, ref, partner))
    advance("kvy")
    for copy in across:
        copy.wait_recv()

    everything = kv_all[...].reshape(n * count, kv_all.shape[2])
    keys, values = everything[:, :DK], everything[:, DK:]
    att_copies = []
    for h in range(0, heads, 2):
        mixes = []
        for i in (h, h + 1):
            scores = lax.dot_general(
                queries[:, i * DK : (i + 1) * DK],
                keys,
                over_rows,
                preferred_element_type=f32,
            )
            exps = jnp.exp(scores - jnp.max(scores, axis=1, keepdims=True))
            norm = jnp.sum(exps, axis=1, keepdims=True)
            mixed = jnp.dot(exps.astype(bf16), values, preferred_element_type=f32)
            mixes.append((mixed / norm).astype(bf16))
        att[0, :, h * DV : (h + 2) * DV] = jnp.concatenate(mixes, axis=1)
        span = pl.ds(h * DV, 2 * DV)
        att_copies.append(remote(att.at[0, :, span], att.at[1, :, span], y_peer))

    advance("mixed")
    for dz in range(nz):
        arrived(O, dz)
    rows_n = count // PAIR_POOL
    features = pair_w.shape[0]
    token_copies = []
    for j in range(Y):
        if j:
            advance("out")
        span = slice(j * count, (j + 1) * count)
        there = pl.ds(j * count, count)
        swaps = []
        for k in range(0, nz, 2):
            acc = 0.0
            for h in range(0, heads, 2):
                if j and not k:
                    att_copies[h // 2].wait_recv()
                across_heads = slice(h * DV, (h + 2) * DV)
                acc = acc + lax.dot_general(
                    o_buf[k : k + 2, :, across_heads].reshape(2 * width, 2 * DV),
                    att[j, :, across_heads],
                    over_rows,
                    preferred_element_type=f32,
                )
            part[1, k : k + 2, :, span] = acc.reshape(2, width, count).astype(bf16)
            both = pl.ds(k, 2)
            swaps.append(
                remote(part.at[1, both, :, there], other.at[1, both, :, there], partner)
            )
        for k in range(0, nz, 2):
            swaps[k // 2].wait_recv()
            columns = slice(k * width, (k + 2) * width)
            pair = [
                emb[b, :, span].astype(f32)
                + (part[1, b, :, span].astype(f32) + other[1, b, :, span].astype(f32))
                for b in (k, k + 1)
            ]
            normed[span, columns] = jnp.concatenate(pair, axis=0).T.astype(bf16)
            if j:
                there = pl.ds(k * width, 2 * width)
                token_copies.append(
                    remote(normed.at[peer_half, there], tok_peer.at[:, there], y_peer)
                )
    row_of = lax.broadcasted_iota(jnp.int32, (2 * rows_n, 2 * count), 0)
    token_of = lax.broadcasted_iota(jnp.int32, (2 * rows_n, 2 * count), 1) // PAIR_POOL
    pool = jnp.where(row_of == token_of, 1.0 / PAIR_POOL, 0.0).astype(bf16)
    for copy in rc_here:
        copy.wait()
    pair_pool = jnp.dot(pool, normed[...], preferred_element_type=f32).astype(bf16)
    projected = jnp.dot(
        pair_pool, rc_buf[...].reshape(nz * width, 2 * features), preferred_element_type=f32
    )
    cols[s] = projected[:, features:].astype(bf16)
    rows_peer[0] = projected[:, :features].astype(bf16)
    rows_copy = remote(rows_peer.at[0], rows_peer.at[1], y_peer)
    col_copies = []
    for d in range(1, n):
        to = {"seq": (s + d) % n}
        col_copies.append(remote(cols.at[s], cols.at[s], to))
    rows_copy.wait_recv()
    row_part = projected[:rows_n, :features] + rows_peer[1].astype(f32)[rows_n:]
    row_part = row_part.astype(bf16).astype(f32)[:, None, :]
    for copy in token_copies:
        copy.wait_recv()
    tok_own, tok_other = normed[own_half, :], tok_peer[...]
    for k in range(nz):
        a = tok_own[:, k * width : (k + 1) * width]
        b = tok_other[:, k * width : (k + 1) * width]
        pair = [jnp.where(y == 0, a, b), jnp.where(y == 0, b, a)]
        tokens_out[:, k * 2 * width : (k + 1) * 2 * width] = jnp.concatenate(pair, axis=1)
    for copy in col_copies:
        copy.wait_recv()
    for j in range(nz // 2):
        both = [cols[c * (n // 2) + Y * j + i].astype(f32) for i in range(Y)]
        for i in range(Y):
            column = both[i][:rows_n] + both[1 - i][rows_n:]
            column = column.astype(bf16).astype(f32)
            hid[:, pl.ds((Y * j + i) * rows_n, rows_n), :] = jax.nn.gelu(
                row_part + column[None, :, :], approximate=True
            )
    hidden = hid[...].reshape(rows_n * (n // 2) * rows_n, features).astype(bf16)
    result = jnp.dot(hidden, pair_w[...], preferred_element_type=f32)
    pair_out[...] = result.reshape(pair_out.shape).astype(bf16)
    for copy in started:
        copy.wait_send()


def hand_over(tokens, pair, tokens_out, pair_out):
    tokens_out[...] = tokens[...]
    pair_out[...] = pair[...]


def on_device_fused(
    signal,
    conv_weight,
    conv_gain,
    embed_weight,
    attn_gain,
    query_weight,
    keyvalue_weight,
    output_weight,
    rowcol_weight,
    pair_weight,
):
    bf16, f32 = jnp.bfloat16, jnp.float32
    n = lax.axis_size("seq")
    nz = n // Y
    positions, half = signal.shape
    taps, channels, _ = conv_weight.shape
    count = positions // POOL
    width = embed_weight.shape[1]
    q_cols = query_weight.shape[1] // 2
    heads = q_cols // DK
    kv_cols = keyvalue_weight.shape[1]
    rows_n = count // PAIR_POOL
    features = pair_weight.shape[0]
    any_spec = pl.BlockSpec(memory_space=pl.ANY)
    vmem = pl.BlockSpec(memory_space=pltpu.VMEM)
    dma = pltpu.SemaphoreType.DMA
    tokens, pair = pl.pallas_call(
        functools.partial(fused_kernel, taps, heads),
        out_shape=(
            jax.ShapeDtypeStruct((count // 2, n * width), bf16),
            jax.ShapeDtypeStruct((rows_n, rows_n * n // 2, features), bf16),
        ),
        in_specs=[any_spec, any_spec, vmem, any_spec, vmem]
        + [any_spec, any_spec, any_spec, any_spec, vmem],
        out_specs=(vmem, vmem),
        scratch_shapes=[
            pltpu.VMEM((2, half, positions), bf16),
            pltpu.VMEM((2, half, positions), bf16),
            pltpu.VMEM((2 * half, taps * count), bf16),
            pltpu.VMEM((EDGE, half), bf16),
            pltpu.VMEM((2, 2, EDGE, half), bf16),
            pltpu.VMEM((taps, half, channels), bf16),
            pltpu.VMEM((nz, width, half), bf16),
            pltpu.VMEM((nz, width, q_cols), bf16),
            pltpu.VMEM((nz, width, kv_cols), bf16),
            pltpu.VMEM((nz, width, heads * DV), bf16),
            pltpu.VMEM((nz, width, 2 * features), bf16),
            pltpu.VMEM((2, half, count), bf16),
            pltpu.VMEM((2, nz, width, 2 * count), bf16),
            pltpu.VMEM((2, nz, width, 2 * count), bf16),
            pltpu.VMEM((nz, width, 2 * count), bf16),
            pltpu.VMEM((2 * count, nz * width), bf16),
            pltpu.VMEM((2, 8, count), f32),
            pltpu.VMEM((count, 128), f32),
            pltpu.VMEM((2, count // 2, kv_cols), bf16),
            pltpu.VMEM((2, count, q_cols), bf16),
            pltpu.VMEM((n, count, kv_cols), bf16),
            pltpu.VMEM((2, count, heads * DV), bf16),
            pltpu.VMEM((count // 2, nz * width), bf16),
            pltpu.VMEM((n, 2 * rows_n, features), bf16),
            pltpu.VMEM((2, 2 * rows_n, features), bf16),
            pltpu.VMEM((n, 1, width), f32),
            pltpu.VMEM((rows_n, rows_n * n // 2, features), f32),
            dma((32,)),
            dma((160,)),
            dma((160,)),
        ],
        compiler_params=pltpu.CompilerParams(
            collective_id=0, has_side_effects=True, vmem_limit_bytes=60 * 1024 * 1024
        ),
    )(
        signal.T,
        jnp.swapaxes(conv_weight, 1, 2),
        conv_gain,
        embed_weight.T,
        attn_gain,
        query_weight,
        keyvalue_weight,
        output_weight.T,
        rowcol_weight,
        pair_weight,
    )
    return pl.pallas_call(
        hand_over,
        out_shape=(
            jax.ShapeDtypeStruct(tokens.shape, bf16),
            jax.ShapeDtypeStruct(pair.shape, bf16),
        ),
        in_specs=[vmem, vmem],
        out_specs=(vmem, vmem),
    )(tokens, pair)


def fits(mesh):
    n = mesh.shape["seq"]
    return n == 8 and mesh.shape["col"] == 2 and mesh.shape["grp"] == 2


def solution(mesh):
    placed = (
        P(("grp", "seq"), "col"),
        P(None, None, "col"),
        P(),
        P("col", "seq"),
        P(),
        P("seq", None),
        P("seq", None),
        P(None, "seq"),
        P(),
        P(),
    )
    return jax.shard_map(
        on_device_fused if fits(mesh) else on_device,
        mesh=mesh,
        in_specs=placed,
        out_specs=(P(("grp", "seq", "col"), None), P(("grp", "seq"), "col", None)),
        check_vma=False,
    )
```

```python
import functools

import jax
import jax.numpy as jnp
from jax import lax
from jax.experimental import pallas as pl
from jax.experimental.pallas import tpu as pltpu
from jax.sharding import PartitionSpec as P

DK = 128
DV = 192
POOL = 4
PAIR_POOL = 16


def with_halo(array, sides, width):
    for axis, dim in sides:
        size, length = (lax.axis_size(axis), array.shape[dim])
        up = [(i, (i + 1) % size) for i in range(size - 1)]
        down = [(j, i) for i, j in up]
        last = lax.slice_in_dim(array, length - width, length, axis=dim)
        first = lax.slice_in_dim(array, 0, width, axis=dim)
        before = lax.ppermute(last, axis, up)
        after = lax.ppermute(first, axis, down)
        array = jnp.concatenate([before, array, after], axis=dim)
    return array


def rms_scale(values, gain_vector):
    return (
        values * lax.rsqrt(jnp.mean(values * values, axis=-1, keepdims=True) + 1e-06) * gain_vector
    )


def attention_parts(queries, head_count):
    query_rows = queries.reshape(queries.shape[0] * head_count, DK)

    def absorb(running, pieces, first_row):
        running_max, running_sum, accumulated = running
        key_piece, value_piece = pieces
        scores = lax.dot_general(
            query_rows, key_piece, (((1,), (1,)), ((), ())), preferred_element_type=jnp.float32
        )
        newest_max = jnp.maximum(running_max, jnp.max(scores, axis=1))
        weights = jnp.exp(scores - newest_max[:, None])
        running_sum = jnp.sum(weights, axis=1)
        accumulated = jnp.dot(
            weights.astype(jnp.bfloat16), value_piece, preferred_element_type=jnp.float32
        )
        return (newest_max, running_sum, accumulated)

    row_count = query_rows.shape[0]
    initial = (
        jnp.full((row_count,), -1e30, jnp.float32),
        jnp.zeros((row_count,), jnp.float32),
        jnp.zeros((row_count, DV), jnp.float32),
    )
    return (absorb, initial)


def finish_attention(result, token_count):
    running_max, running_sum, accumulated = result
    return (accumulated / running_sum[:, None]).astype(jnp.bfloat16).reshape(token_count, -1)


def on_device(
    signal,
    conv_weight,
    conv_gain,
    embed_weight,
    attn_gain,
    query_weight,
    keyvalue_weight,
    output_weight,
    rowcol_weight,
    pair_weight,
):
    positions = signal.shape[0]
    tap_count = conv_weight.shape[0]
    halo_width = tap_count // 2
    padded = with_halo(signal, (("seq", 0),), halo_width)
    widened = lax.all_gather(padded, "col", axis=1, tiled=True)
    activated = jax.nn.gelu(
        rms_scale(widened.astype(jnp.float32), conv_gain), approximate=True
    ).astype(jnp.bfloat16)
    summed = signal.astype(jnp.float32)
    for tap_index in range(tap_count):
        summed = summed + jnp.dot(
            activated[tap_index : tap_index + positions],
            conv_weight[tap_index],
            preferred_element_type=jnp.float32,
        )
    pooled = jnp.mean(summed.reshape(positions // POOL, POOL, -1), axis=1).astype(jnp.bfloat16)
    embed_full = lax.all_gather(embed_weight, "seq", axis=1, tiled=True)
    col_count = lax.axis_size("col")
    embedded = lax.psum_scatter(
        jnp.dot(pooled, embed_full, preferred_element_type=jnp.float32).astype(jnp.bfloat16),
        "col",
        scatter_dimension=0,
        tiled=True,
    )
    normed = rms_scale(embedded.astype(jnp.float32), attn_gain).astype(jnp.bfloat16)
    head_count = query_weight.shape[1] // DK
    scaling = DK ** (-0.5)
    col_index = lax.axis_index("col")
    local_heads = head_count // col_count
    group_tokens = lax.all_gather(normed, "col", axis=0, tiled=True)
    group_count = group_tokens.shape[0]
    query_half = lax.dynamic_slice_in_dim(
        query_weight, col_index * local_heads * DK, local_heads * DK, 1
    )
    query_sum = jnp.dot(
        group_tokens,
        lax.all_gather(query_half, "seq", axis=0, tiled=True),
        preferred_element_type=jnp.float32,
    )
    keyvalue_sum = jnp.dot(
        group_tokens,
        lax.all_gather(keyvalue_weight, "seq", axis=0, tiled=True),
        preferred_element_type=jnp.float32,
    )
    queries = (query_sum * scaling).astype(jnp.bfloat16)
    keyvalue = keyvalue_sum.astype(jnp.bfloat16)
    absorb, initial = attention_parts(queries, local_heads)
    result = absorb(
        initial,
        (
            lax.all_gather(keyvalue[:, :DK], "seq", axis=0, tiled=True),
            lax.all_gather(keyvalue[:, DK:], "seq", axis=0, tiled=True),
        ),
        jnp.int32(0),
    )
    attended = finish_attention(result, group_count)
    output_half = lax.dynamic_slice_in_dim(
        output_weight, col_index * local_heads * DV, local_heads * DV, 0
    )
    partial_out = jnp.dot(
        attended,
        lax.all_gather(output_half, "seq", axis=1, tiled=True),
        preferred_element_type=jnp.float32,
    )
    attention_out = lax.psum_scatter(
        partial_out.astype(jnp.bfloat16), "col", scatter_dimension=0, tiled=True
    ).astype(jnp.float32)
    tokens = (embedded.astype(jnp.float32) + attention_out).astype(jnp.bfloat16)
    pair_pool = jnp.mean(
        tokens.astype(jnp.float32).reshape(-1, PAIR_POOL, tokens.shape[1]), axis=1
    ).astype(jnp.bfloat16)
    projected = jnp.dot(pair_pool, rowcol_weight, preferred_element_type=jnp.float32).astype(
        jnp.bfloat16
    )
    features = pair_weight.shape[0]
    row_block = lax.all_gather(projected, "col", axis=0, tiled=True)
    column_all = lax.all_gather(row_block[:, features:], "seq", axis=0, tiled=True)
    row_part = row_block[:, :features]
    column_span = column_all.shape[0] // col_count
    column_part = lax.dynamic_slice_in_dim(
        column_all, lax.axis_index("col") * column_span, column_span, 0
    )
    hidden = jax.nn.gelu(
        row_part.astype(jnp.float32)[:, None, :] + column_part.astype(jnp.float32)[None, :, :],
        approximate=True,
    ).astype(jnp.bfloat16)
    pair_out = jnp.dot(
        hidden.reshape(-1, features), pair_weight, preferred_element_type=jnp.float32
    ).astype(jnp.bfloat16)
    return (tokens, pair_out.reshape(row_part.shape[0], column_span, features))


EDGE = 16
Y = 2
PIECES = (3, 1, 2, 2)
E, KV, Q, O = range(4)
ORDER = (0, 1, 3, 2)
PLAN = {
    "start": ((E,), (KV,),),
    "act": ((E, 1, 0),),
    "edges": ((E, 1, 1),),
    "mean": ((E, 1, 2), (E, 3, 0),),
    "win": ((E, 3, 1), (E, 3, 2), (KV, 1), (Q,),),
    ("conv", 0): ((E, 2, 0),),
    ("conv", 2): ((E, 2, 1), (KV, 3),),
    "wait": ((E, 2, 2), (KV, 2), (Q, 1),),
    ("pass", 0): ((O,),),
    ("swap", 0): ((Q, 3),),
    ("swap", 2): ((Q, 2),),
    "kv": ((O, 1), (O, 3),),
    "query": ((O, 2),),
}


def fused_kernel(
    taps,
    heads,
    signal,
    conv_w,
    conv_gain,
    embed_w,
    attn_gain,
    query_w,
    kv_w,
    out_w,
    rowcol,
    pair_w,
    tokens_out,
    pair_out,
    sig,
    act,
    win,
    edge,
    halo,
    conv_buf,
    e_buf,
    q_buf,
    k_buf,
    o_buf,
    rc_buf,
    pools,
    part,
    other,
    emb,
    normed,
    ssq,
    scales,
    kv_part,
    q_part,
    kv_all,
    att,
    tok_peer,
    cols,
    rows_peer,
    gain_buf,
    hid,
    loc_sem,
    send_sem,
    recv_sem,
):
    f32, bf16 = jnp.float32, jnp.bfloat16
    n = lax.axis_size("seq")
    nz = n // Y
    s = lax.axis_index("seq")
    c = lax.axis_index("col")
    x = lax.axis_index("grp")
    z, y = s // Y, s % Y
    half = sig.shape[1]
    positions = sig.shape[2]
    count = positions // POOL
    width = e_buf.shape[1]
    halo_width = taps // 2
    started = []
    local = []

    def remote(src, dst, to):
        index = len(started)
        copy = pltpu.make_async_remote_copy(
            src_ref=src,
            dst_ref=dst,
            send_sem=send_sem.at[index],
            recv_sem=recv_sem.at[index],
            device_id=to,
            device_id_type=pl.DeviceIdType.MESH,
        )
        copy.start()
        started.append(copy)
        return copy

    def fetch(src, dst):
        copy = pltpu.make_async_copy(src, dst, loc_sem.at[len(local)])
        copy.start()
        local.append(copy)
        return copy

    def seq_of(z_index, y_index):
        return z_index * Y + y_index

    def z_from(dz):
        return (z + nz - dz) % nz

    def z_to(dz):
        return (z + dz) % nz

    partner = {"col": 1 - c}
    y_peer = {"seq": seq_of(z, 1 - y)}
    x_peer = {"grp": 1 - x}
    z_next = {"seq": seq_of(z_to(1), y)}

    sig_here = fetch(signal, sig.at[0])
    barrier = pltpu.get_barrier_semaphore()
    for d in range(n):
        for e in range(2):
            if d or e:
                pl.semaphore_signal(
                    barrier,
                    inc=1,
                    device_id={"seq": (s + d) % n, "col": (c + e) % 2},
                    device_id_type=pl.DeviceIdType.MESH,
                )
    pl.semaphore_signal(barrier, inc=1, device_id=x_peer, device_id_type=pl.DeviceIdType.MESH)

    k_rows = kv_w.shape[0] // 2
    q_cols = query_w.shape[1] // 2
    o_cols = out_w.shape[1] // 2
    kv_own = kv_w.at[pl.ds(pl.multiple_of(c * k_rows, 16), k_rows)]
    q_own = query_w.at[:, pl.ds(pl.multiple_of(c * q_cols, 128), q_cols)]
    o_own = out_w.at[:, pl.ds(pl.multiple_of(c * o_cols, 128), o_cols)]

    def k_at(owner):
        return k_buf.at[owner, pl.ds(pl.multiple_of(c * k_rows, 16), k_rows)]

    weights = [
        (embed_w, lambda owner: e_buf.at[owner]),
        (kv_own, k_at),
        (q_own, lambda owner: q_buf.at[owner]),
        (o_own, lambda owner: o_buf.at[owner]),
    ]
    conv_here = [fetch(conv_w.at[t], conv_buf.at[t]) for t in range(taps)]
    own_here = [fetch(own, at(z)) for own, at in weights]
    rc_here = []
    for k in range(nz):
        rows = pl.ds(pl.multiple_of(seq_of(k, y) * width, 16), width)
        rc_here.append(fetch(rowcol.at[rows], rc_buf.at[k]))

    row = lax.broadcasted_iota(jnp.int32, (EDGE, positions), 0)
    place = lax.broadcasted_iota(jnp.int32, (EDGE, positions), 1)
    wanted = jnp.where(row < EDGE // 2, row, row - EDGE // 2 + positions - halo_width)
    in_use = lax.rem(row, EDGE // 2) < halo_width
    pick = jnp.where((place == wanted) & in_use, 1.0, 0.0).astype(bf16)
    sig_here.wait()
    over_rows = (((1,), (1,)), ((), ()))
    edge[...] = lax.dot_general(pick, sig[0], over_rows, preferred_element_type=f32).astype(bf16)

    pl.semaphore_wait(barrier, 2 * n)

    signal_copy = remote(signal, sig.at[1], partner)
    copies = {}

    def piece(ref, w, p):
        rows = ref.shape[0] // 2 // PIECES[w]
        return ref.at[pl.ds(pl.multiple_of((x * PIECES[w] + p) * rows, 16), rows)]

    def begin(w, far=(1, 3)):
        own, at = weights[w]
        for p in range(PIECES[w]):
            for dz in far:
                to = {"seq": seq_of(z_to(dz), y)}
                copies[w, p, "z", dz] = remote(piece(own, w, p), piece(at(z), w, p), to)

    def hop(w, dz, p=None):
        _, at = weights[w]
        for p in range(PIECES[w]) if p is None else (p,):
            copies[w, p, "z", dz].wait_recv()
            ref = piece(at(z_from(dz)), w, p)
            if dz + 1 < nz and (w, p, "z", dz + 1) not in copies:
                copies[w, p, "z", dz + 1] = remote(ref, ref, z_next)
            copies[w, p, "x", dz] = remote(ref, ref, x_peer)

    def advance(point):
        for step in PLAN.get(point, ()):
            begin(step[0]) if len(step) == 1 else hop(*step)

    def arrived(w, dz):
        if dz == 0:
            own_here[w].wait()
        else:
            for p in range(PIECES[w]):
                copies[w, p, "x", dz].wait_recv()

    halo_copies = []
    for e in range(2):
        core = (c + e) % 2
        up = {"seq": (s + 1) % n, "col": core}
        down = {"seq": (s + n - 1) % n, "col": core}
        halo_copies.append(remote(edge, halo.at[e, 0], up))
        halo_copies.append(remote(edge, halo.at[e, 1], down))
    advance("start")

    def windows(position):
        column = lax.broadcasted_iota(jnp.int32, position.shape, 1)
        tap = column // count
        begin = (column - tap * count) * POOL + tap - halo_width
        hit = (position >= begin) & (position < begin + POOL)
        return jnp.where(hit, 1.0 / POOL, 0.0).astype(bf16)

    mean_of = windows(lax.broadcasted_iota(jnp.int32, (positions, taps * count), 0))
    edge_row = lax.broadcasted_iota(jnp.int32, (EDGE, taps * count), 0)
    edge_means = [windows(edge_row - EDGE // 2 - halo_width), windows(edge_row + positions)]
    edge_means = [
        jnp.where((edge_row >= EDGE // 2) & (s > 0), edge_means[0], 0.0).astype(bf16),
        jnp.where((edge_row < EDGE // 2) & (s < n - 1), edge_means[1], 0.0).astype(bf16),
    ]
    channels = 2 * half
    gain_row = conv_gain[...].reshape(1, channels)
    gains = [gain_row[:, :half], gain_row[:, half:]]
    gains = [jnp.where(c == h, gains[0], gains[1]) for h in range(2)]
    gain_columns = [jnp.broadcast_to(g, (128, half)).T for g in gains]

    signal_copy.wait_recv()

    block = 64
    square = jnp.zeros((1, positions), f32)
    for h in range(2):
        v = sig[h].astype(f32)
        square = square + jnp.sum(v * v, axis=0, keepdims=True)
    scale = lax.rsqrt(square * (1.0 / channels) + 1e-06)
    for h in range(2):
        if h:
            advance("half")
        for i in range(half // block):
            rows = slice(i * block, (i + 1) * block)
            v = sig[h, rows, :].astype(f32) * scale * gain_columns[h][rows, :1]
            act[h, rows, :] = jax.nn.gelu(v, approximate=True).astype(bf16)

    advance("act")
    for copy in halo_copies:
        copy.wait_recv()

    edges = [[], []]
    for side in range(2):
        a, b = halo[0, side].astype(f32), halo[1, side].astype(f32)
        square = jnp.sum(a * a, axis=1, keepdims=True) + jnp.sum(b * b, axis=1, keepdims=True)
        edge_scale = lax.rsqrt(square * (1.0 / channels) + 1e-06)
        for h, v in enumerate((a, b)):
            v = jax.nn.gelu(v * edge_scale * gains[h], approximate=True)
            edges[h].append(v.T.astype(bf16))
    advance("edges")
    for h in range(2):
        if h:
            advance("mean")
        core = c if h == 0 else 1 - c
        mean = jnp.dot(act[h], mean_of, preferred_element_type=f32)
        for side in range(2):
            mean = mean + jnp.dot(edges[h][side], edge_means[side], preferred_element_type=f32)
        win[pl.ds(pl.multiple_of(core * half, 16), half), :] = mean.astype(bf16)

    advance("win")

    middle = slice(halo_width * count, (halo_width + 1) * count)
    for copy in conv_here:
        copy.wait()
    chunks = 4
    size = half // chunks
    pool_copies = []
    for i in range(chunks):
        rows = slice(i * size, (i + 1) * size)
        total = jnp.dot(sig[0, rows, :], mean_of[:, middle], preferred_element_type=f32)
        for t in range(taps):
            if t == halo_width:
                advance(("tap", i))
            total = total + jnp.dot(
                conv_buf[t, rows, :],
                win[:, t * count : (t + 1) * count],
                preferred_element_type=f32,
            )
        pools[0, rows, :] = total.astype(bf16)
        span = pl.ds(i * size, size)
        pool_copies.append(remote(pools.at[0, span], pools.at[1, span], y_peer))
        advance(("conv", i))

    gain_row = attn_gain[...].reshape(1, n * width)
    for k in range(n):
        gain_buf[k] = gain_row[:, k * width : (k + 1) * width]
    own_half = pl.ds(pl.multiple_of(c * (count // 2), 16), count // 2)
    peer_half = pl.ds(pl.multiple_of(count + c * (count // 2), 16), count // 2)
    advance("wait")
    for copy in pool_copies:
        copy.wait_recv()
    both = jnp.concatenate([pools[0], pools[1]], axis=1)
    square = jnp.zeros((1, 2 * count), f32)
    kv = 0.0
    for k in range(0, nz, 2):
        order = ORDER[k : k + 2]
        owners = [z_from(dz) for dz in order]
        swaps = []
        for dz, owner in zip(order, owners):
            advance(("owner", dz))
            arrived(E, dz)
            part[0, owner] = jnp.dot(e_buf[owner], both, preferred_element_type=f32).astype(bf16)
            swaps.append(remote(part.at[0, owner], other.at[0, owner], partner))
        for dz, owner in zip(order, owners):
            advance(("pass", dz))
            arrived(KV, dz)
            ref = k_at(owner)
            swaps.append(remote(ref, ref, partner))
        for copy in swaps[:2]:
            copy.wait_recv()
        advance(("swap", k))
        pair = []
        for owner in owners:
            v = (part[0, owner].astype(f32) + other[0, owner].astype(f32)).astype(bf16)
            emb[owner] = v
            v = v.astype(f32)
            square = square + jnp.sum(v * v, axis=0, keepdims=True)
            pair.append(v)
        gain = jnp.concatenate([gain_buf[seq_of(owner, y)] for owner in owners], axis=1)
        columns = slice(k * width, (k + 2) * width)
        normed[:, columns] = (jnp.concatenate(pair, axis=0).T * gain).astype(bf16)
        for copy in swaps[2:]:
            copy.wait_recv()
        kv = kv + jnp.dot(
            jnp.concatenate([normed[own_half, columns], normed[peer_half, columns]], axis=0),
            jnp.concatenate([k_buf[owner] for owner in owners], axis=0),
            preferred_element_type=f32,
        )
    kv_part[0] = kv[count // 2 :].astype(bf16)
    kv_swap = remote(kv_part.at[0], kv_part.at[1], y_peer)
    ssq[0] = jnp.broadcast_to(square[:, count:], (8, count))
    ssq_copy = remote(ssq.at[0], ssq.at[1], y_peer)

    advance("kv")
    ssq_copy.wait_recv()
    square = square[:, :count] + ssq[1, 0:1, :]
    scale = lax.rsqrt(square * (1.0 / (n * width)) + 1e-06)
    scales[...] = jnp.broadcast_to(scale, (128, count)).T

    def kv_at(owner):
        return kv_all.at[owner, own_half]

    kv_swap.wait_recv()
    kv = (kv[: count // 2] + kv_part[1].astype(f32)) * scales[own_half, :1]
    kv_all[s, own_half, :] = kv.astype(bf16)
    mine = kv_at(s)
    kv_copies = {}
    for dz in (2, 1, 3):
        kv_copies["z", dz] = remote(mine, mine, {"seq": seq_of(z_to(dz), y)})
    kv_copies["y", 0] = remote(mine, mine, y_peer)
    across = [remote(mine, mine, partner)]
    advance("sent")
    for dz in range(nz):
        arrived(Q, dz)
    queries = jnp.dot(
        normed[...],
        jnp.concatenate([q_buf[z_from(dz)] for dz in ORDER], axis=0),
        preferred_element_type=f32,
    )
    q_part[0] = queries[count:].astype(bf16)
    q_swap = remote(q_part.at[0], q_part.at[1], y_peer)

    advance("query")
    q_swap.wait_recv()
    queries = (queries[:count] + q_part[1].astype(f32)) * (scales[:, :1] * (DK**-0.5))
    queries = queries.astype(bf16)
    for dz in (1, 3, 2):
        advance(("z", dz))
        kv_copies["z", dz].wait_recv()
        ref = kv_at(seq_of(z_from(dz), y))
        kv_copies["y", dz] = remote(ref, ref, y_peer)
        across.append(remote(ref, ref, partner))
    for dz in (0, 1, 3, 2):
        advance(("y", dz))
        kv_copies["y", dz].wait_recv()
        ref = kv_at(seq_of(z_from(dz), 1 - y))
        across.append(remote(ref, ref, partner))
    advance("kvy")
    for copy in across:
        copy.wait_recv()

    everything = kv_all[...].reshape(n * count, kv_all.shape[2])
    keys, values = everything[:, :DK], everything[:, DK:]
    att_copies = []
    for h in range(0, heads, 2):
        mixes = []
        for i in (h, h + 1):
            scores = lax.dot_general(
                queries[:, i * DK : (i + 1) * DK],
                keys,
                over_rows,
                preferred_element_type=f32,
            )
            exps = jnp.exp(scores - jnp.max(scores, axis=1, keepdims=True))
            norm = jnp.sum(exps, axis=1, keepdims=True)
            mixed = jnp.dot(exps.astype(bf16), values, preferred_element_type=f32)
            mixes.append((mixed / norm).astype(bf16))
        att[0, :, h * DV : (h + 2) * DV] = jnp.concatenate(mixes, axis=1)
        span = pl.ds(h * DV, 2 * DV)
        att_copies.append(remote(att.at[0, :, span], att.at[1, :, span], y_peer))

    advance("mixed")
    for dz in range(nz):
        arrived(O, dz)
    rows_n = count // PAIR_POOL
    features = pair_w.shape[0]
    token_copies = []
    for j in range(Y):
        if j:
            advance("out")
        span = slice(j * count, (j + 1) * count)
        there = pl.ds(j * count, count)
        swaps = []
        for k in range(0, nz, 2):
            acc = 0.0
            for h in range(0, heads, 2):
                if j and not k:
                    att_copies[h // 2].wait_recv()
                across_heads = slice(h * DV, (h + 2) * DV)
                acc = acc + lax.dot_general(
                    o_buf[k : k + 2, :, across_heads].reshape(2 * width, 2 * DV),
                    att[j, :, across_heads],
                    over_rows,
                    preferred_element_type=f32,
                )
            part[1, k : k + 2, :, span] = acc.reshape(2, width, count).astype(bf16)
            both = pl.ds(k, 2)
            swaps.append(
                remote(part.at[1, both, :, there], other.at[1, both, :, there], partner)
            )
        for k in range(0, nz, 2):
            swaps[k // 2].wait_recv()
            columns = slice(k * width, (k + 2) * width)
            pair = [
                emb[b, :, span].astype(f32)
                + (part[1, b, :, span].astype(f32) + other[1, b, :, span].astype(f32))
                for b in (k, k + 1)
            ]
            normed[span, columns] = jnp.concatenate(pair, axis=0).T.astype(bf16)
            if j:
                there = pl.ds(k * width, 2 * width)
                token_copies.append(
                    remote(normed.at[peer_half, there], tok_peer.at[:, there], y_peer)
                )
    row_of = lax.broadcasted_iota(jnp.int32, (2 * rows_n, 2 * count), 0)
    token_of = lax.broadcasted_iota(jnp.int32, (2 * rows_n, 2 * count), 1) // PAIR_POOL
    pool = jnp.where(row_of == token_of, 1.0 / PAIR_POOL, 0.0).astype(bf16)
    for copy in rc_here:
        copy.wait()
    pair_pool = jnp.dot(pool, normed[...], preferred_element_type=f32).astype(bf16)
    projected = jnp.dot(
        pair_pool, rc_buf[...].reshape(nz * width, 2 * features), preferred_element_type=f32
    )
    cols[s] = projected[:, features:].astype(bf16)
    rows_peer[0] = projected[:, :features].astype(bf16)
    rows_copy = remote(rows_peer.at[0], rows_peer.at[1], y_peer)
    col_copies = []
    for d in range(1, n):
        to = {"seq": (s + d) % n}
        col_copies.append(remote(cols.at[s], cols.at[s], to))
    rows_copy.wait_recv()
    row_part = projected[:rows_n, :features] + rows_peer[1].astype(f32)[rows_n:]
    row_part = row_part.astype(bf16).astype(f32)[:, None, :]
    for copy in token_copies:
        copy.wait_recv()
    tok_own, tok_other = normed[own_half, :], tok_peer[...]
    for k in range(nz):
        a = tok_own[:, k * width : (k + 1) * width]
        b = tok_other[:, k * width : (k + 1) * width]
        pair = [jnp.where(y == 0, a, b), jnp.where(y == 0, b, a)]
        tokens_out[:, k * 2 * width : (k + 1) * 2 * width] = jnp.concatenate(pair, axis=1)
    for copy in col_copies:
        copy.wait_recv()
    for j in range(nz // 2):
        both = [cols[c * (n // 2) + Y * j + i].astype(f32) for i in range(Y)]
        for i in range(Y):
            column = both[i][:rows_n] + both[1 - i][rows_n:]
            column = column.astype(bf16).astype(f32)
            hid[:, pl.ds((Y * j + i) * rows_n, rows_n), :] = jax.nn.gelu(
                row_part + column[None, :, :], approximate=True
            )
    hidden = hid[...].reshape(rows_n * (n // 2) * rows_n, features).astype(bf16)
    result = jnp.dot(hidden, pair_w[...], preferred_element_type=f32)
    pair_out[...] = result.reshape(pair_out.shape).astype(bf16)
    for copy in started:
        copy.wait_send()


def hand_over(tokens, pair, tokens_out, pair_out):
    tokens_out[...] = tokens[...]
    pair_out[...] = pair[...]


def on_device_fused(
    signal,
    conv_weight,
    conv_gain,
    embed_weight,
    attn_gain,
    query_weight,
    keyvalue_weight,
    output_weight,
    rowcol_weight,
    pair_weight,
):
    bf16, f32 = jnp.bfloat16, jnp.float32
    n = lax.axis_size("seq")
    nz = n // Y
    positions, half = signal.shape
    taps, channels, _ = conv_weight.shape
    count = positions // POOL
    width = embed_weight.shape[1]
    q_cols = query_weight.shape[1] // 2
    heads = q_cols // DK
    kv_cols = keyvalue_weight.shape[1]
    rows_n = count // PAIR_POOL
    features = pair_weight.shape[0]
    any_spec = pl.BlockSpec(memory_space=pl.ANY)
    vmem = pl.BlockSpec(memory_space=pltpu.VMEM)
    dma = pltpu.SemaphoreType.DMA
    tokens, pair = pl.pallas_call(
        functools.partial(fused_kernel, taps, heads),
        out_shape=(
            jax.ShapeDtypeStruct((count // 2, n * width), bf16),
            jax.ShapeDtypeStruct((rows_n, rows_n * n // 2, features), bf16),
        ),
        in_specs=[any_spec, any_spec, vmem, any_spec, vmem]
        + [any_spec, any_spec, any_spec, any_spec, vmem],
        out_specs=(vmem, vmem),
        scratch_shapes=[
            pltpu.VMEM((2, half, positions), bf16),
            pltpu.VMEM((2, half, positions), bf16),
            pltpu.VMEM((2 * half, taps * count), bf16),
            pltpu.VMEM((EDGE, half), bf16),
            pltpu.VMEM((2, 2, EDGE, half), bf16),
            pltpu.VMEM((taps, half, channels), bf16),
            pltpu.VMEM((nz, width, half), bf16),
            pltpu.VMEM((nz, width, q_cols), bf16),
            pltpu.VMEM((nz, width, kv_cols), bf16),
            pltpu.VMEM((nz, width, heads * DV), bf16),
            pltpu.VMEM((nz, width, 2 * features), bf16),
            pltpu.VMEM((2, half, count), bf16),
            pltpu.VMEM((2, nz, width, 2 * count), bf16),
            pltpu.VMEM((2, nz, width, 2 * count), bf16),
            pltpu.VMEM((nz, width, 2 * count), bf16),
            pltpu.VMEM((2 * count, nz * width), bf16),
            pltpu.VMEM((2, 8, count), f32),
            pltpu.VMEM((count, 128), f32),
            pltpu.VMEM((2, count // 2, kv_cols), bf16),
            pltpu.VMEM((2, count, q_cols), bf16),
            pltpu.VMEM((n, count, kv_cols), bf16),
            pltpu.VMEM((2, count, heads * DV), bf16),
            pltpu.VMEM((count // 2, nz * width), bf16),
            pltpu.VMEM((n, 2 * rows_n, features), bf16),
            pltpu.VMEM((2, 2 * rows_n, features), bf16),
            pltpu.VMEM((n, 1, width), f32),
            pltpu.VMEM((rows_n, rows_n * n // 2, features), f32),
            dma((32,)),
            dma((160,)),
            dma((160,)),
        ],
        compiler_params=pltpu.CompilerParams(
            collective_id=0, has_side_effects=True, vmem_limit_bytes=60 * 1024 * 1024
        ),
    )(
        signal.T,
        jnp.swapaxes(conv_weight, 1, 2),
        conv_gain,
        embed_weight.T,
        attn_gain,
        query_weight,
        keyvalue_weight,
        output_weight.T,
        rowcol_weight,
        pair_weight,
    )
    return pl.pallas_call(
        hand_over,
        out_shape=(
            jax.ShapeDtypeStruct(tokens.shape, bf16),
            jax.ShapeDtypeStruct(pair.shape, bf16),
        ),
        in_specs=[vmem, vmem],
        out_specs=(vmem, vmem),
    )(tokens, pair)


def fits(mesh):
    n = mesh.shape["seq"]
    return n == 8 and mesh.shape["col"] == 2 and mesh.shape["grp"] == 2


def solution(mesh):
    placed = (
        P(("grp", "seq"), "col"),
        P(None, None, "col"),
        P(),
        P("col", "seq"),
        P(),
        P("seq", None),
        P("seq", None),
        P(None, "seq"),
        P(),
        P(),
    )
    return jax.shard_map(
        on_device_fused if fits(mesh) else on_device,
        mesh=mesh,
        in_specs=placed,
        out_specs=(P(("grp", "seq", "col"), None), P(("grp", "seq"), "col", None)),
        check_vma=False,
    )
```
